32 devices in a mesh: grp: 2 (over x), res: 16 (over z, y, core).
Axes of the slice: x: 2, y: 2, z: 4, core: 2. Of those that a mesh axis runs over, the one named last changes fastest.
Arguments:
- stacked_sequence_embedding: bfloat16 [1024, 8192], P(('grp', 'res')), parts along dimension 0, may hold values from -6 to 6
- normalizer_multiplier: float32 [64], replicated, may hold values from 0.1 to 1.9
- normalizer_additive: float32 [64], replicated, may hold values from -2 to 2
- lhs_projected_tensor: bfloat16 [64, 32], replicated, may hold values from -0.75 to 0.75
- rhs_projected_tensor: bfloat16 [64, 32], replicated, may hold values from -0.75 to 0.75
- pairwise_matrix: bfloat16 [1024, 128], replicated, may hold values from -0.359375 to 0.359375
- pairwise_shift: float32 [128], replicated, may hold values from -3 to 3
Outputs:
- pair_update: bfloat16 [256, 128, 128], P(('grp', 'res')), parts along dimension 0
The draws below stay inside these ranges and needn't reach their ends.
There are 2 independent parts, one for each index of `grp`. The reference program is written for one: setup_inputs(seed, part) draws one part's arguments, and reference() takes and returns one part's arrays. A program takes and returns all parts, laid end to end along the dimension named above; an argument that names none is the same for every part. Nothing has to cross between parts.
All inputs are finite; a program needn't handle non-finite values.
Results may differ from the reference program's by a relative error of at most 0.0047.
Values may be sent and summed in bfloat16 or wider, within the bound.
A program may use at most 128 MiB of HBM per device.

```python
import jax
import jax.numpy as jnp
from jax import lax

ROW_CHANNEL_SIZE = 64
HIDDEN_WIDTH = 32
C_Z = 128
R_DEV = 8
RELATED_SEQS = 512
PROTEIN_SPAN = 128


def shard_levels(rng, dims, shards, least, top_value):
    def one(axis_at, blocks):
        heights = jax.random.uniform(jax.random.fold_in(jax.random.fold_in(rng, 6), axis_at), (blocks,), jnp.float32, least / len(shards), top_value / len(shards))
        return jnp.repeat(jnp.exp(heights), dims[axis_at] // blocks).reshape((-1,) + (1,) * (len(dims) - axis_at - 1))

    level = one(*shards[0])
    for cut in shards[1:]:
        level = level * one(*cut)
    return level


def centred(own_key, extent, width, most, shards=(), dtype=jnp.bfloat16):
    level = shard_levels(own_key, extent, shards, -0.22, 0.18) if shards else 1.0
    values = jax.random.normal(own_key, extent, jnp.float32) * width * level
    return jnp.minimum(jnp.maximum(values, -most), most).astype(dtype)


def setup_inputs(seed: int = 0, part: int = 0) -> dict:
    arg_keys = jax.random.split(jax.random.key(seed), 8)
    part_keys = jax.random.split(jax.random.fold_in(arg_keys[7], part), 8)
    stacked_sequence_embedding = centred(part_keys[0], (RELATED_SEQS, PROTEIN_SPAN * ROW_CHANNEL_SIZE), 1.0, 6.0, ((0, 16),))
    normalizer_multiplier = jnp.clip(1.0 + 0.18 * jax.random.normal(arg_keys[1], (ROW_CHANNEL_SIZE,), jnp.float32), 0.1, 1.9)
    normalizer_additive = centred(arg_keys[2], (ROW_CHANNEL_SIZE,), 0.4, 2.0, (), jnp.float32)
    lhs_projected_tensor = centred(arg_keys[3], (ROW_CHANNEL_SIZE, HIDDEN_WIDTH), ROW_CHANNEL_SIZE ** -0.5, 0.75)
    rhs_projected_tensor = centred(arg_keys[4], (ROW_CHANNEL_SIZE, HIDDEN_WIDTH), ROW_CHANNEL_SIZE ** -0.5, 0.75)
    pairwise_matrix = centred(arg_keys[5], (HIDDEN_WIDTH * HIDDEN_WIDTH, C_Z), 0.06, 0.359375)
    pairwise_shift = centred(arg_keys[6], (C_Z,), 0.5, 3.0, (), jnp.float32)
    return {"stacked_sequence_embedding": stacked_sequence_embedding, "normalizer_multiplier": normalizer_multiplier, "normalizer_additive": normalizer_additive, "lhs_projected_tensor": lhs_projected_tensor, "rhs_projected_tensor": rhs_projected_tensor, "pairwise_matrix": pairwise_matrix, "pairwise_shift": pairwise_shift}


def normalize(member_list, normalizer_multiplier, normalizer_additive):
    center = member_list - lax.optimization_barrier(jnp.mean(member_list, axis=-1, keepdims=True))
    spread = lax.optimization_barrier(jnp.mean(center * center, axis=-1, keepdims=True))
    return (center * lax.rsqrt(spread + 1e-05) * normalizer_multiplier + normalizer_additive).astype(jnp.bfloat16)

def reference(stacked_sequence_embedding, normalizer_multiplier, normalizer_additive, lhs_projected_tensor, rhs_projected_tensor, pairwise_matrix, pairwise_shift):
    member_list = stacked_sequence_embedding.astype(jnp.float32).reshape(RELATED_SEQS * PROTEIN_SPAN, ROW_CHANNEL_SIZE)
    normed = normalize(member_list, normalizer_multiplier, normalizer_additive)
    left = jnp.dot(normed, lhs_projected_tensor, preferred_element_type=jnp.float32).astype(jnp.bfloat16).reshape(RELATED_SEQS, PROTEIN_SPAN * HIDDEN_WIDTH)
    right = jnp.dot(normed, rhs_projected_tensor, preferred_element_type=jnp.float32).astype(jnp.bfloat16).reshape(RELATED_SEQS, PROTEIN_SPAN * HIDDEN_WIDTH)
    left_blocks = left.reshape(RELATED_SEQS, PROTEIN_SPAN // R_DEV, R_DEV * HIDDEN_WIDTH).transpose(1, 0, 2)

    def one_block(block):
        outer = lax.dot_general(block.astype(jnp.float32), right.astype(jnp.float32), (((0,), (0,)), ((), ()))) / RELATED_SEQS
        flat = outer.reshape(R_DEV, HIDDEN_WIDTH, PROTEIN_SPAN, HIDDEN_WIDTH).transpose(0, 2, 1, 3).reshape(R_DEV * PROTEIN_SPAN, HIDDEN_WIDTH * HIDDEN_WIDTH).astype(jnp.bfloat16)
        mapped = jnp.dot(flat, pairwise_matrix, preferred_element_type=jnp.float32) + pairwise_shift
        return mapped.astype(jnp.bfloat16).reshape(R_DEV, PROTEIN_SPAN, C_Z)
    tiles = lax.map(one_block, left_blocks)
    return tiles.reshape(PROTEIN_SPAN, PROTEIN_SPAN, C_Z)
```

```python
import functools

import jax
import jax.numpy as jnp
from jax import lax
from jax.experimental import pallas as pl
from jax.experimental.pallas import tpu as pltpu
from jax.sharding import PartitionSpec as P

F32 = jnp.float32
BF16 = jnp.bfloat16
LANES = 128
WAVES = 4
BY_Y = 4


def dot(a, b):
    return jnp.dot(a, b, preferred_element_type=F32)


def kernel(
    n,
    x_ref,
    gain_ref,
    offset_ref,
    lhs_ref,
    rhs_ref,
    pair_ref,
    shift_ref,
    out_ref,
    norm_scr,
    turn_scr,
    pair_scr,
    pair_t,
    left_send,
    left_all,
    left_t,
    right_all,
    flat,
    mix,
    kept,
    sum_send,
    sum_recv,
    l_send,
    l_recv,
    own_send,
    own_recv,
    y_send,
    y_recv,
    z_send,
    z_recv,
    peer_send,
    peer_recv,
    s_send,
    s_recv,
):
    rows = x_ref.shape[0]
    width, chans = lhs_ref.shape
    residues = x_ref.shape[1] // chans
    resid = residues // n
    tiles = x_ref.shape[1] // LANES
    per_tile = LANES // chans
    team = n // 2
    across = team // 4
    me = lax.axis_index("res")
    half = me // team
    seat = lax.rem(me, team)
    core = lax.rem(seat, 2)
    y = lax.rem(seat // 2, 2)
    z = seat // 4
    base = half * team
    partner = (1 - half) * team + seat
    peer_seat = seat + 1 - 2 * core

    def to(dev):
        return dict(device_id={"res": dev}, device_id_type=pl.DeviceIdType.MESH)

    def seat_at(z_step, flip, c):
        return lax.rem(z + z_step + across, across) * 4 + (1 - y if flip else y) * 2 + c

    barrier = pltpu.get_barrier_semaphore()

    def over(first, last, act):
        def step(k, carry):
            act(k)
            return carry

        lax.fori_loop(first, last, step, 0)

    over(1, team, lambda k: pl.semaphore_signal(barrier, inc=1, **to(base + lax.rem(seat + k, team))))
    pl.semaphore_signal(barrier, inc=1, **to(partner))

    def same(shape, down, across):
        r = lax.broadcasted_iota(jnp.int32, shape, 0) // down
        c = lax.broadcasted_iota(jnp.int32, shape, 1) // across
        return r == c

    reps = LANES // width
    lhs = jnp.concatenate([lhs_ref[...].astype(F32)] * per_tile, axis=1)
    lhs = jnp.concatenate([lhs] * reps, axis=0).T
    lhs_wide = jnp.concatenate([lhs] * (reps // per_tile), axis=0)
    lhs_wide = jnp.where(same(lhs_wide.shape, chans, width), lhs_wide, 0.0).astype(BF16)
    fold = width // WAVES
    rhs = rhs_ref[...].astype(F32)
    rhs_t = jnp.concatenate(
        [
            jnp.concatenate([rhs[k * fold : (k + 1) * fold] for k in (2 * g, 2 * g + 1)], axis=1)
            for g in range(WAVES // 2)
        ],
        axis=0,
    ).astype(BF16)
    averager = jnp.where(same((LANES, LANES), chans, chans), 1.0 / chans, 0.0).astype(BF16)
    gain = jnp.concatenate([gain_ref[...]] * per_tile, axis=1)
    offset = jnp.concatenate([offset_ref[...]] * per_tile, axis=1)

    group = 8
    dests = group * per_tile // resid
    halves = resid * width // LANES
    groups = tiles // 2 // group

    def project(b, which):
        start = ((half if which else 1 - half) * groups + b) * group
        x = jnp.concatenate(
            [
                x_ref[:, pl.ds(pl.multiple_of((start + u) * LANES, LANES), LANES)].astype(F32)
                for u in range(group)
            ],
            axis=0,
        )
        center = x - dot(x.astype(BF16), averager)
        square = center * center
        high = square.astype(BF16)
        low = (square - high.astype(F32)).astype(BF16)
        spread = dot(high, averager) + dot(low, averager)
        normed = (center * lax.rsqrt(spread + 1e-05) * gain + offset).astype(BF16)
        wide = normed.astype(F32)
        at = (which * groups + b) * group * rows
        norm_scr[pl.ds(pl.multiple_of(at, 8), group * rows), :] = wide
        even = jnp.concatenate(
            [wide[u * rows : (u + 1) * rows] for u in range(0, group, 2)], axis=0
        ).astype(BF16)
        odd = jnp.concatenate(
            [wide[u * rows : (u + 1) * rows] for u in range(1, group, 2)], axis=0
        ).astype(BF16)
        left = dot(jnp.concatenate([even, odd], axis=1), lhs_wide)
        for u in range(group // 2):
            left_send[
                which, b * dests + u // halves, :, (u % halves) * LANES : (u % halves + 1) * LANES
            ] = left[u * rows : (u + 1) * rows].astype(BF16)

    def left_copy(k, which, incoming):
        slot = team - k if incoming else k
        other = lax.rem(seat + k, team)
        return pltpu.make_async_remote_copy(
            src_ref=left_send.at[which, other],
            dst_ref=left_all.at[which, other if incoming else seat],
            send_sem=l_send.at[which, slot],
            recv_sem=l_recv.at[which, slot],
            **to(base + other),
        )

    part = fold * residues
    cut = part // LANES * BY_Y // 8 * LANES

    def own(w, k, incoming):
        z_step = 0 if isinstance(k, int) else (-k if incoming else k)
        flip = isinstance(k, int)
        other = seat_at(z_step, flip, core)
        ref = right_all.at[w, other if incoming else seat]
        return pltpu.make_async_remote_copy(
            src_ref=ref,
            dst_ref=ref,
            send_sem=own_send.at[w, k],
            recv_sem=own_recv.at[w, k],
            **to(base + other),
        )

    def relay_y(w, k, incoming):
        source = seat_at(-k, incoming, core)
        ref = right_all.at[w, source, :, pl.ds(0, cut)]
        return pltpu.make_async_remote_copy(
            src_ref=ref,
            dst_ref=ref,
            send_sem=y_send.at[w, k],
            recv_sem=y_recv.at[w, k],
            **to(base + seat_at(0, True, core)),
        )

    def relay_z(w, k, incoming):
        source = seat_at(-k if incoming else 0, True, core)
        ref = right_all.at[w, source, :, pl.ds(cut, part - cut)]
        return pltpu.make_async_remote_copy(
            src_ref=ref,
            dst_ref=ref,
            send_sem=z_send.at[w, k],
            recv_sem=z_recv.at[w, k],
            **to(base + seat_at(-k if incoming else k, False, core)),
        )

    def share(w, k, kind, incoming):
        source = seat_at(-k, kind > 0, 1 - core if incoming else core)
        ref = right_all.at[w, source]
        if kind == 1:
            ref = right_all.at[w, source, :, pl.ds(0, cut)]
        if kind == 2:
            ref = right_all.at[w, source, :, pl.ds(cut, part - cut)]
        return pltpu.make_async_remote_copy(
            src_ref=ref,
            dst_ref=ref,
            send_sem=peer_send.at[w, kind, k],
            recv_sem=peer_recv.at[w, kind, k],
            **to(base + peer_seat),
        )

    def share_near(w, incoming):
        source = seat_at(0, True, 1 - core if incoming else core)
        ref = right_all.at[w, source]
        return pltpu.make_async_remote_copy(
            src_ref=ref,
            dst_ref=ref,
            send_sem=peer_send.at[w, 1, 0],
            recv_sem=peer_recv.at[w, 1, 0],
            **to(base + peer_seat),
        )

    lane = lax.broadcasted_iota(jnp.int32, (tiles // WAVES, LANES), 1) // chans
    strips = residues // LANES
    wave_tiles = tiles // WAVES
    span = residues // WAVES
    batch = 8
    fold_lane = lax.broadcasted_iota(jnp.int32, (fold, LANES), 1) // (LANES // 2)

    def turn(b, w):
        ones = [
            norm_scr[pl.ds(w * wave_tiles * rows + b * batch + v, wave_tiles, stride=rows), :]
            for v in range(batch)
        ]
        picked = []
        for one in ones:
            rolled = pltpu.roll(one, chans, 1)
            picked += [jnp.where(lane == q, one if q == h else rolled, 0.0) for q in range(2) for h in range(2)]
        spread_out = jnp.concatenate(picked, axis=0).astype(BF16)
        res = lax.dot_general(
            rhs_t, spread_out, (((1,), (1,)), ((), ())), preferred_element_type=F32
        )
        deep = residues // 2

        def put(v, j, value):
            turn_scr[w * strips + j, pl.ds(b * batch + v, fold, stride=rows), :] = value

        if deep % LANES:
            for v in range(0, batch, 2):
                low = res[:fold, v * deep : v * deep + LANES]
                high = res[fold:, v * deep : v * deep + LANES]
                put(v, 0, jnp.where(fold_lane == 0, low, pltpu.roll(high, LANES // 2, 1)))
                put(v + 1, 0, jnp.where(fold_lane == 0, pltpu.roll(low, LANES // 2, 1), high))
        else:
            for v in range(batch):
                for j in range(strips):
                    g, at = j * LANES // deep, v * deep + j * LANES % deep
                    put(v, j, res[g * fold : (g + 1) * fold, at : at + LANES])

    def turned(w):
        over(0, rows // batch, lambda b: turn(b, w))
        for q in range(fold):
            for j in range(strips):
                at = q * residues + j * LANES
                right_all[w, seat, :, at : at + LANES] = turn_scr[
                    w * strips + j, q * rows : (q + 1) * rows, :
                ].astype(BF16)

    def give(w):
        own(w, 0, False).start()
        over(1, across, lambda k: own(w, k, False).start())
        share(w, 0, 0, False).start()

    def relay(w):
        def along(k):
            own(w, k, True).wait_recv()
            relay_y(w, k, False).start()
            share(w, k, 0, False).start()

        own(w, 0, True).wait_recv()
        over(1, across, lambda k: relay_z(w, k, False).start())
        share_near(w, False).start()
        over(1, across, along)

    def pass_on(w):
        def along(k):
            relay_y(w, k, True).wait_recv()
            share(w, k, 1, False).start()
            relay_z(w, k, True).wait_recv()
            share(w, k, 2, False).start()

        over(1, across, along)

    def gathered(w):
        over(0, across, lambda k: share(w, k, 0, True).wait_recv())
        share_near(w, True).wait_recv()

        def along(k):
            share(w, k, 1, True).wait_recv()
            share(w, k, 2, True).wait_recv()

        over(1, across, along)

    out_chans = pair_ref.shape[1]

    def prepare():
        pair_scr[...] = pair_ref[...].astype(F32)
        for c in range(WAVES):
            for b in range(fold // reps):
                some = jnp.concatenate(
                    [
                        pair_scr[pl.ds(c * fold + b * reps + u, width, stride=width), :]
                        for u in range(reps)
                    ],
                    axis=0,
                )
                pair_t[c * out_chans : (c + 1) * out_chans, b * LANES : (b + 1) * LANES] = (
                    some.T.astype(BF16)
                )

    qs = 4
    here_rows = team * rows
    total = n * rows
    slot = lax.broadcasted_iota(jnp.int32, (out_chans, residues), 1) // span

    def fill(which, w):
        for b in range(fold // qs):
            here = right_all[w, :, :, b * qs * residues : (b + 1) * qs * residues]
            if rows % 16:
                here = here.astype(F32)
            here = here.reshape(here_rows, qs * residues).astype(BF16)
            product = (dot(left_t[which], here) * (1.0 / total)).astype(BF16)
            for u in range(qs):
                for i in range(resid):
                    flat[
                        (b * qs + u) * width : (b * qs + u + 1) * width,
                        i * residues : (i + 1) * residues,
                    ] = product[i * width : (i + 1) * width, u * residues : (u + 1) * residues]

    def sums(b, w):
        return pltpu.make_async_remote_copy(
            src_ref=sum_send.at[w, b],
            dst_ref=sum_recv.at[w, b],
            send_sem=s_send.at[w, b],
            recv_sem=s_recv.at[w, b],
            **to(partner),
        )

    def mapped(b):
        both = dot(
            pair_t[...], flat[:, b * WAVES * residues : (b + 1) * WAVES * residues]
        )
        whole = None
        for d in range(WAVES):
            one = None
            for q in range(WAVES):
                i = (q + d) % WAVES
                piece = both[q * out_chans : (q + 1) * out_chans, i * residues : (i + 1) * residues]
                one = piece if one is None else jnp.where(slot == q, piece, one)
            if d:
                one = pltpu.roll(one, d * span, 1)
            whole = one if whole is None else whole + one
        return whole

    blocks = resid // WAVES

    def theirs(w):
        fill(0, w)
        for b in range(blocks):
            sum_send[w, b] = mapped(b).astype(BF16)
            sums(b, w).start()

    def mine(w):
        fill(1, w)
        for b in range(blocks):
            kept[w, b] = mapped(b)

    def finish(r):
        w = (r + WAVES // 2) % WAVES
        first = (half if 2 * w >= WAVES else 1 - half) * (residues // 2) + w % (WAVES // 2) * span
        for b in range(blocks):
            sums(b, r).wait_recv()
            done = (kept[w, b] + sum_recv[r, b].astype(F32)).T + shift_ref[...]
            for u in range(WAVES):
                for h in range(2):
                    at = u * span + h * wave_tiles
                    mix[WAVES * b + u, pl.ds(first + h, wave_tiles, stride=2), :] = done[
                        at : at + wave_tiles
                    ]
        rows_at = pl.ds(pl.multiple_of(first, span), span)
        for i in range(resid):
            out_ref[i, rows_at, :] = mix[i, rows_at, :].astype(BF16)

    def left_turn(which):
        over(1, team, lambda k: left_copy(k, which, True).wait_recv())
        left_t[which] = (
            left_all[which].astype(F32).reshape(team * rows, resid * width).T.astype(BF16)
        )

    def left_give(which):
        over(1, team, lambda k: left_copy(k, which, False).start())
        left_all[which, seat] = left_send[which, seat]

    over(0, groups, lambda b: project(b, 0))
    pl.semaphore_wait(barrier, team)
    left_give(0)
    turned(0)
    give(0)
    turned(1)
    give(1)
    over(0, groups, lambda b: project(b, 1))
    left_give(1)
    relay(0)
    turned(2)
    give(2)
    relay(1)
    turned(3)
    give(3)
    pass_on(0)
    prepare()
    left_turn(0)
    gathered(0)
    theirs(0)
    relay(2)
    pass_on(1)
    gathered(1)
    theirs(1)
    relay(3)
    pass_on(2)
    gathered(2)
    theirs(2)
    pass_on(3)
    gathered(3)
    theirs(3)
    left_turn(1)
    mine(0)
    mine(1)
    mine(2)
    finish(0)
    mine(3)
    finish(1)
    finish(2)
    finish(3)

    for w in range(WAVES):
        own(w, 0, False).wait_send()
        over(1, across, lambda k: own(w, k, False).wait_send())
        over(1, across, lambda k: relay_y(w, k, False).wait_send())
        over(1, across, lambda k: relay_z(w, k, False).wait_send())
        over(0, across, lambda k: share(w, k, 0, False).wait_send())
        share_near(w, False).wait_send()
        over(1, across, lambda k: share(w, k, 1, False).wait_send())
        over(1, across, lambda k: share(w, k, 2, False).wait_send())
        for b in range(blocks):
            sums(b, w).wait_send()
    for which in range(2):
        over(1, team, lambda k: left_copy(k, which, False).wait_send())


def on_device(n, x, gain, offset, lhs, rhs, pair, shift):
    rows = x.shape[0]
    chans, width = lhs.shape
    residues = x.shape[1] // chans
    resid = residues // n
    tiles = x.shape[1] // LANES
    team = n // 2
    across = team // 4
    depth = width * width
    out_chans = pair.shape[1]
    blocks = resid // WAVES
    fold = width // WAVES
    vmem = pl.BlockSpec(memory_space=pltpu.VMEM)
    return pl.pallas_call(
        functools.partial(kernel, n),
        out_shape=jax.ShapeDtypeStruct((resid, residues, out_chans), BF16),
        in_specs=[vmem] * 7,
        out_specs=vmem,
        scratch_shapes=[
            pltpu.VMEM((tiles * rows, LANES), F32),
            pltpu.VMEM((WAVES * residues // LANES, fold * rows, LANES), F32),
            pltpu.VMEM((depth, out_chans), F32),
            pltpu.VMEM((WAVES * out_chans, depth // WAVES), BF16),
            pltpu.VMEM((2, team, rows, resid * width), BF16),
            pltpu.VMEM((2, team, rows, resid * width), BF16),
            pltpu.VMEM((2, resid * width, team * rows), BF16),
            pltpu.VMEM((WAVES, team, rows, fold * residues), BF16),
            pltpu.VMEM((depth // WAVES, resid * residues), BF16),
            pltpu.VMEM((resid, residues, out_chans), F32),
            pltpu.VMEM((WAVES, blocks, out_chans, residues), F32),
            pltpu.VMEM((WAVES, blocks, out_chans, residues), BF16),
            pltpu.VMEM((WAVES, blocks, out_chans, residues), BF16),
            pltpu.SemaphoreType.DMA((2, team)),
            pltpu.SemaphoreType.DMA((2, team)),
            pltpu.SemaphoreType.DMA((WAVES, across)),
            pltpu.SemaphoreType.DMA((WAVES, across)),
            pltpu.SemaphoreType.DMA((WAVES, across)),
            pltpu.SemaphoreType.DMA((WAVES, across)),
            pltpu.SemaphoreType.DMA((WAVES, across)),
            pltpu.SemaphoreType.DMA((WAVES, across)),
            pltpu.SemaphoreType.DMA((WAVES, 3, across)),
            pltpu.SemaphoreType.DMA((WAVES, 3, across)),
            pltpu.SemaphoreType.DMA((WAVES, blocks)),
            pltpu.SemaphoreType.DMA((WAVES, blocks)),
        ],
        compiler_params=pltpu.CompilerParams(
            collective_id=0, has_side_effects=True, vmem_limit_bytes=56 * 1024 * 1024
        ),
    )(x, gain.reshape(1, -1), offset.reshape(1, -1), lhs.T, rhs.T, pair, shift.reshape(1, -1))


def solution(mesh):
    in_specs = (P(("grp", "res"), None), P(), P(), P(), P(), P(), P())
    out_specs = P(("grp", "res"), None, None)
    return jax.shard_map(
        functools.partial(on_device, mesh.shape["res"]),
        mesh=mesh,
        in_specs=in_specs,
        out_specs=out_specs,
        check_vma=False,
    )
```

```python
import functools

import jax
import jax.numpy as jnp
from jax import lax
from jax.experimental import pallas as pl
from jax.experimental.pallas import tpu as pltpu
from jax.sharding import PartitionSpec as P

F32 = jnp.float32
BF16 = jnp.bfloat16
LANES = 128
WAVES = 4
BY_Y = 4


def dot(a, b):
    return jnp.dot(a, b, preferred_element_type=F32)


def kernel(
    n,
    x_hbm,
    gain_hbm,
    offset_hbm,
    lhs_hbm,
    rhs_hbm,
    pair_hbm,
    out_ref,
    x_ref,
    gain_ref,
    offset_ref,
    lhs_ref,
    rhs_ref,
    pair_ref,
    in_sem,
    norm_scr,
    turn_scr,
    pair_scr,
    pair_t,
    left_send,
    left_all,
    left_t,
    right_all,
    flat,
    kept,
    sum_send,
    sum_recv,
    l_send,
    l_recv,
    own_send,
    own_recv,
    y_send,
    y_recv,
    z_send,
    z_recv,
    peer_send,
    peer_recv,
    s_send,
    s_recv,
):
    rows = x_ref.shape[0]
    width, chans = lhs_ref.shape
    residues = x_ref.shape[1] // chans
    resid = residues // n
    tiles = x_ref.shape[1] // LANES
    per_tile = LANES // chans
    team = n // 2
    across = team // 4
    me = lax.axis_index("res")
    half = me // team
    seat = lax.rem(me, team)
    core = lax.rem(seat, 2)
    y = lax.rem(seat // 2, 2)
    z = seat // 4
    base = half * team
    partner = (1 - half) * team + seat
    peer_seat = seat + 1 - 2 * core

    def to(dev):
        return dict(device_id={"res": dev}, device_id_type=pl.DeviceIdType.MESH)

    def seat_at(z_step, flip, c):
        return lax.rem(z + z_step + across, across) * 4 + (1 - y if flip else y) * 2 + c

    barrier = pltpu.get_barrier_semaphore()

    def over(first, last, act):
        def step(k, carry):
            act(k)
            return carry

        lax.fori_loop(first, last, step, 0)

    over(1, team, lambda k: pl.semaphore_signal(barrier, inc=1, **to(base + lax.rem(seat + k, team))))
    pl.semaphore_signal(barrier, inc=1, **to(partner))

    def load(k, source, target):
        copy = pltpu.make_async_copy(source, target, in_sem.at[k])
        copy.start()
        return copy

    def x_half(which):
        wide = x_ref.shape[1] // 2
        at = pl.ds(pl.multiple_of((half if which else 1 - half) * wide, LANES), wide)
        return x_hbm.at[:, at], x_ref.at[:, at]

    small = [
        load(0, gain_hbm, gain_ref),
        load(1, offset_hbm, offset_ref),
        load(2, lhs_hbm, lhs_ref),
        load(3, rhs_hbm, rhs_ref),
    ]
    x_in = [load(4, *x_half(0)), load(5, *x_half(1))]
    pair_in = load(6, pair_hbm, pair_ref)
    for copy in small:
        copy.wait()

    def same(shape, down, across):
        r = lax.broadcasted_iota(jnp.int32, shape, 0) // down
        c = lax.broadcasted_iota(jnp.int32, shape, 1) // across
        return r == c

    reps = LANES // width
    lhs = jnp.concatenate([lhs_ref[...].astype(F32)] * per_tile, axis=1)
    lhs = jnp.concatenate([lhs] * reps, axis=0).T
    lhs_wide = jnp.concatenate([lhs] * (reps // per_tile), axis=0)
    lhs_wide = jnp.where(same(lhs_wide.shape, chans, width), lhs_wide, 0.0).astype(BF16)
    fold = width // WAVES
    rhs = rhs_ref[...].astype(F32)
    rhs_t = jnp.concatenate(
        [
            jnp.concatenate([rhs[k * fold : (k + 1) * fold] for k in (2 * g, 2 * g + 1)], axis=1)
            for g in range(WAVES // 2)
        ],
        axis=0,
    ).astype(BF16)
    averager = jnp.where(same((LANES, LANES), chans, chans), 1.0 / chans, 0.0).astype(BF16)
    gain = jnp.concatenate([gain_ref[...]] * per_tile, axis=1)
    offset = jnp.concatenate([offset_ref[...]] * per_tile, axis=1)

    group = 8
    dests = group * per_tile // resid
    halves = resid * width // LANES
    groups = tiles // 2 // group

    def project(b, which):
        start = ((half if which else 1 - half) * groups + b) * group
        x = jnp.concatenate(
            [
                x_ref[:, pl.ds(pl.multiple_of((start + u) * LANES, LANES), LANES)].astype(F32)
                for u in range(group)
            ],
            axis=0,
        )
        center = x - dot(x.astype(BF16), averager)
        square = center * center
        high = square.astype(BF16)
        low = (square - high.astype(F32)).astype(BF16)
        spread = dot(high, averager) + dot(low, averager)
        normed = (center * lax.rsqrt(spread + 1e-05) * gain + offset).astype(BF16)
        wide = normed.astype(F32)
        at = (which * groups + b) * group * rows
        norm_scr[pl.ds(pl.multiple_of(at, 8), group * rows), :] = wide
        even = jnp.concatenate(
            [wide[u * rows : (u + 1) * rows] for u in range(0, group, 2)], axis=0
        ).astype(BF16)
        odd = jnp.concatenate(
            [wide[u * rows : (u + 1) * rows] for u in range(1, group, 2)], axis=0
        ).astype(BF16)
        left = dot(jnp.concatenate([even, odd], axis=1), lhs_wide)
        for u in range(group // 2):
            left_send[
                which, b * dests + u // halves, :, (u % halves) * LANES : (u % halves + 1) * LANES
            ] = left[u * rows : (u + 1) * rows].astype(BF16)

    def left_copy(k, which, incoming):
        slot = team - k if incoming else k
        other = lax.rem(seat + k, team)
        return pltpu.make_async_remote_copy(
            src_ref=left_send.at[which, other],
            dst_ref=left_all.at[which, other if incoming else seat],
            send_sem=l_send.at[which, slot],
            recv_sem=l_recv.at[which, slot],
            **to(base + other),
        )

    part = fold * residues
    cut = part // LANES * BY_Y // 8 * LANES

    def own(w, k, incoming):
        z_step = 0 if isinstance(k, int) else (-k if incoming else k)
        flip = isinstance(k, int)
        other = seat_at(z_step, flip, core)
        ref = right_all.at[w, other if incoming else seat]
        return pltpu.make_async_remote_copy(
            src_ref=ref,
            dst_ref=ref,
            send_sem=own_send.at[w, k],
            recv_sem=own_recv.at[w, k],
            **to(base + other),
        )

    def relay_y(w, k, incoming):
        source = seat_at(-k, incoming, core)
        ref = right_all.at[w, source, :, pl.ds(0, cut)]
        return pltpu.make_async_remote_copy(
            src_ref=ref,
            dst_ref=ref,
            send_sem=y_send.at[w, k],
            recv_sem=y_recv.at[w, k],
            **to(base + seat_at(0, True, core)),
        )

    def relay_z(w, k, incoming):
        source = seat_at(-k if incoming else 0, True, core)
        ref = right_all.at[w, source, :, pl.ds(cut, part - cut)]
        return pltpu.make_async_remote_copy(
            src_ref=ref,
            dst_ref=ref,
            send_sem=z_send.at[w, k],
            recv_sem=z_recv.at[w, k],
            **to(base + seat_at(-k if incoming else k, False, core)),
        )

    def share(w, k, kind, incoming):
        source = seat_at(-k, kind > 0, 1 - core if incoming else core)
        ref = right_all.at[w, source]
        if kind == 1:
            ref = right_all.at[w, source, :, pl.ds(0, cut)]
        if kind == 2:
            ref = right_all.at[w, source, :, pl.ds(cut, part - cut)]
        return pltpu.make_async_remote_copy(
            src_ref=ref,
            dst_ref=ref,
            send_sem=peer_send.at[w, kind, k],
            recv_sem=peer_recv.at[w, kind, k],
            **to(base + peer_seat),
        )

    def share_near(w, incoming):
        source = seat_at(0, True, 1 - core if incoming else core)
        ref = right_all.at[w, source]
        return pltpu.make_async_remote_copy(
            src_ref=ref,
            dst_ref=ref,
            send_sem=peer_send.at[w, 1, 0],
            recv_sem=peer_recv.at[w, 1, 0],
            **to(base + peer_seat),
        )

    lane = lax.broadcasted_iota(jnp.int32, (tiles // WAVES, LANES), 1) // chans
    strips = residues // LANES
    wave_tiles = tiles // WAVES
    span = residues // WAVES
    batch = 8
    fold_lane = lax.broadcasted_iota(jnp.int32, (fold, LANES), 1) // (LANES // 2)

    def turn(b, w):
        ones = [
            norm_scr[pl.ds(w * wave_tiles * rows + b * batch + v, wave_tiles, stride=rows), :]
            for v in range(batch)
        ]
        picked = []
        for one in ones:
            rolled = pltpu.roll(one, chans, 1)
            picked += [jnp.where(lane == q, one if q == h else rolled, 0.0) for q in range(2) for h in range(2)]
        spread_out = jnp.concatenate(picked, axis=0).astype(BF16)
        res = lax.dot_general(
            rhs_t, spread_out, (((1,), (1,)), ((), ())), preferred_element_type=F32
        )
        deep = residues // 2

        def put(v, j, value):
            turn_scr[w * strips + j, pl.ds(b * batch + v, fold, stride=rows), :] = value

        if deep % LANES:
            for v in range(0, batch, 2):
                low = res[:fold, v * deep : v * deep + LANES]
                high = res[fold:, v * deep : v * deep + LANES]
                put(v, 0, jnp.where(fold_lane == 0, low, pltpu.roll(high, LANES // 2, 1)))
                put(v + 1, 0, jnp.where(fold_lane == 0, pltpu.roll(low, LANES // 2, 1), high))
        else:
            for v in range(batch):
                for j in range(strips):
                    g, at = j * LANES // deep, v * deep + j * LANES % deep
                    put(v, j, res[g * fold : (g + 1) * fold, at : at + LANES])

    def turned(w):
        over(0, rows // batch, lambda b: turn(b, w))
        for q in range(fold):
            for j in range(strips):
                at = q * residues + j * LANES
                right_all[w, seat, :, at : at + LANES] = turn_scr[
                    w * strips + j, q * rows : (q + 1) * rows, :
                ].astype(BF16)

    def give(w):
        own(w, 0, False).start()
        over(1, across, lambda k: own(w, k, False).start())
        share(w, 0, 0, False).start()

    def relay(w):
        def along(k):
            own(w, k, True).wait_recv()
            relay_y(w, k, False).start()
            share(w, k, 0, False).start()

        own(w, 0, True).wait_recv()
        over(1, across, lambda k: relay_z(w, k, False).start())
        share_near(w, False).start()
        over(1, across, along)

    def pass_on(w):
        def along(k):
            relay_y(w, k, True).wait_recv()
            share(w, k, 1, False).start()
            relay_z(w, k, True).wait_recv()
            share(w, k, 2, False).start()

        over(1, across, along)

    def gathered(w):
        over(0, across, lambda k: share(w, k, 0, True).wait_recv())
        share_near(w, True).wait_recv()

        def along(k):
            share(w, k, 1, True).wait_recv()
            share(w, k, 2, True).wait_recv()

        over(1, across, along)

    out_chans = pair_ref.shape[1]

    def prepare():
        pair_in.wait()
        pair_scr[...] = pair_ref[...].astype(F32)
        for c in range(WAVES):
            for b in range(fold // reps):
                some = jnp.concatenate(
                    [
                        pair_scr[pl.ds(c * fold + b * reps + u, width, stride=width), :]
                        for u in range(reps)
                    ],
                    axis=0,
                )
                pair_t[c * out_chans : (c + 1) * out_chans, b * LANES : (b + 1) * LANES] = (
                    some.T.astype(BF16)
                )

    qs = 4
    here_rows = team * rows
    total = n * rows
    slot = lax.broadcasted_iota(jnp.int32, (out_chans, residues), 1) // span

    def fill(which, w):
        for b in range(fold // qs):
            here = right_all[w, :, :, b * qs * residues : (b + 1) * qs * residues]
            if rows % 16:
                here = here.astype(F32)
            here = here.reshape(here_rows, qs * residues).astype(BF16)
            product = (dot(left_t[which], here) * (1.0 / total)).astype(BF16)
            for u in range(qs):
                for i in range(resid):
                    flat[
                        (b * qs + u) * width : (b * qs + u + 1) * width,
                        i * residues : (i + 1) * residues,
                    ] = product[i * width : (i + 1) * width, u * residues : (u + 1) * residues]

    def sums(b, w):
        return pltpu.make_async_remote_copy(
            src_ref=sum_send.at[w, b],
            dst_ref=sum_recv.at[w, b],
            send_sem=s_send.at[w, b],
            recv_sem=s_recv.at[w, b],
            **to(partner),
        )

    def mapped(b):
        both = dot(
            pair_t[...], flat[:, b * WAVES * residues : (b + 1) * WAVES * residues]
        )
        whole = None
        for d in range(WAVES):
            one = None
            for q in range(WAVES):
                i = (q + d) % WAVES
                piece = both[q * out_chans : (q + 1) * out_chans, i * residues : (i + 1) * residues]
                one = piece if one is None else jnp.where(slot == q, piece, one)
            if d:
                one = pltpu.roll(one, d * span, 1)
            whole = one if whole is None else whole + one
        return whole

    blocks = resid // WAVES

    def theirs(w):
        fill(0, w)
        for b in range(blocks):
            sum_send[w, b] = mapped(b).astype(BF16)
            sums(b, w).start()

    def mine(w):
        fill(1, w)
        for b in range(blocks):
            kept[w, b] = mapped(b)

    def finish(r):
        w = (r + WAVES // 2) % WAVES
        first = (half if 2 * w >= WAVES else 1 - half) * (residues // 2) + w % (WAVES // 2) * span
        for b in range(blocks):
            sums(b, r).wait_recv()
            done = (kept[w, b] + sum_recv[r, b].astype(F32)).T
            for u in range(WAVES):
                for h in range(2):
                    at = u * span + h * wave_tiles
                    out_ref[WAVES * b + u, pl.ds(first + h, wave_tiles, stride=2), :] = done[
                        at : at + wave_tiles
                    ]

    def left_turn(which):
        over(1, team, lambda k: left_copy(k, which, True).wait_recv())
        left_t[which] = (
            left_all[which].astype(F32).reshape(team * rows, resid * width).T.astype(BF16)
        )

    def left_give(which):
        over(1, team, lambda k: left_copy(k, which, False).start())
        left_all[which, seat] = left_send[which, seat]

    x_in[0].wait()
    over(0, groups, lambda b: project(b, 0))
    pl.semaphore_wait(barrier, team)
    left_give(0)
    turned(0)
    give(0)
    turned(1)
    give(1)
    x_in[1].wait()
    over(0, groups, lambda b: project(b, 1))
    left_give(1)
    relay(0)
    turned(2)
    give(2)
    relay(1)
    turned(3)
    give(3)
    pass_on(0)
    prepare()
    left_turn(0)
    gathered(0)
    theirs(0)
    relay(2)
    pass_on(1)
    gathered(1)
    theirs(1)
    relay(3)
    pass_on(2)
    gathered(2)
    theirs(2)
    pass_on(3)
    gathered(3)
    theirs(3)
    left_turn(1)
    mine(0)
    mine(1)
    mine(2)
    finish(0)
    mine(3)
    finish(1)
    finish(2)
    finish(3)

    for w in range(WAVES):
        own(w, 0, False).wait_send()
        over(1, across, lambda k: own(w, k, False).wait_send())
        over(1, across, lambda k: relay_y(w, k, False).wait_send())
        over(1, across, lambda k: relay_z(w, k, False).wait_send())
        over(0, across, lambda k: share(w, k, 0, False).wait_send())
        share_near(w, False).wait_send()
        over(1, across, lambda k: share(w, k, 1, False).wait_send())
        over(1, across, lambda k: share(w, k, 2, False).wait_send())
        for b in range(blocks):
            sums(b, w).wait_send()
    for which in range(2):
        over(1, team, lambda k: left_copy(k, which, False).wait_send())


def on_device(n, x, gain, offset, lhs, rhs, pair, shift):
    rows = x.shape[0]
    chans, width = lhs.shape
    residues = x.shape[1] // chans
    resid = residues // n
    tiles = x.shape[1] // LANES
    team = n // 2
    across = team // 4
    depth = width * width
    out_chans = pair.shape[1]
    blocks = resid // WAVES
    fold = width // WAVES
    vmem = pl.BlockSpec(memory_space=pltpu.VMEM)
    args = [
        pltpu.with_memory_space_constraint(v, pltpu.HBM)
        for v in (x, gain.reshape(1, -1), offset.reshape(1, -1), lhs.T, rhs.T, pair)
    ]
    out = pl.pallas_call(
        functools.partial(kernel, n),
        out_shape=pltpu.VMEM((resid, residues, out_chans), F32),
        in_specs=[pl.BlockSpec(memory_space=pltpu.HBM)] * 6,
        out_specs=vmem,
        scratch_shapes=[
            pltpu.VMEM(x.shape, BF16),
            pltpu.VMEM((1, chans), F32),
            pltpu.VMEM((1, chans), F32),
            pltpu.VMEM((width, chans), BF16),
            pltpu.VMEM((width, chans), BF16),
            pltpu.VMEM(pair.shape, BF16),
            pltpu.SemaphoreType.DMA((7,)),
            pltpu.VMEM((tiles * rows, LANES), F32),
            pltpu.VMEM((WAVES * residues // LANES, fold * rows, LANES), F32),
            pltpu.VMEM((depth, out_chans), F32),
            pltpu.VMEM((WAVES * out_chans, depth // WAVES), BF16),
            pltpu.VMEM((2, team, rows, resid * width), BF16),
            pltpu.VMEM((2, team, rows, resid * width), BF16),
            pltpu.VMEM((2, resid * width, team * rows), BF16),
            pltpu.VMEM((WAVES, team, rows, fold * residues), BF16),
            pltpu.VMEM((depth // WAVES, resid * residues), BF16),
            pltpu.VMEM((WAVES, blocks, out_chans, residues), F32),
            pltpu.VMEM((WAVES, blocks, out_chans, residues), BF16),
            pltpu.VMEM((WAVES, blocks, out_chans, residues), BF16),
            pltpu.SemaphoreType.DMA((2, team)),
            pltpu.SemaphoreType.DMA((2, team)),
            pltpu.SemaphoreType.DMA((WAVES, across)),
            pltpu.SemaphoreType.DMA((WAVES, across)),
            pltpu.SemaphoreType.DMA((WAVES, across)),
            pltpu.SemaphoreType.DMA((WAVES, across)),
            pltpu.SemaphoreType.DMA((WAVES, across)),
            pltpu.SemaphoreType.DMA((WAVES, across)),
            pltpu.SemaphoreType.DMA((WAVES, 3, across)),
            pltpu.SemaphoreType.DMA((WAVES, 3, across)),
            pltpu.SemaphoreType.DMA((WAVES, blocks)),
            pltpu.SemaphoreType.DMA((WAVES, blocks)),
        ],
        compiler_params=pltpu.CompilerParams(
            collective_id=0, has_side_effects=True, vmem_limit_bytes=40 * 1024 * 1024
        ),
    )(*args)
    return (out + shift).astype(BF16)


def solution(mesh):
    in_specs = (P(("grp", "res"), None), P(), P(), P(), P(), P(), P())
    out_specs = P(("grp", "res"), None, None)
    return jax.shard_map(
        functools.partial(on_device, mesh.shape["res"]),
        mesh=mesh,
        in_specs=in_specs,
        out_specs=out_specs,
        check_vma=False,
    )
```

```python
import functools

import jax
import jax.numpy as jnp
from jax import lax
from jax.experimental import pallas as pl
from jax.experimental.pallas import tpu as pltpu
from jax.sharding import PartitionSpec as P

F32 = jnp.float32
BF16 = jnp.bfloat16
LANES = 128
WAVES = 4
BY_Y = 4
DIRECT = 1


def dot(a, b):
    return jnp.dot(a, b, preferred_element_type=F32)


def kernel(
    n,
    x_hbm,
    gain_hbm,
    offset_hbm,
    lhs_hbm,
    rhs_hbm,
    pair_hbm,
    out_ref,
    x_ref,
    gain_ref,
    offset_ref,
    lhs_ref,
    rhs_ref,
    pair_ref,
    in_sem,
    norm_scr,
    turn_scr,
    pair_scr,
    pair_t,
    left_send,
    left_all,
    left_t,
    right_all,
    flat,
    kept,
    sum_send,
    sum_recv,
    l_send,
    l_recv,
    own_send,
    own_recv,
    y_send,
    y_recv,
    z_send,
    z_recv,
    peer_send,
    peer_recv,
    s_send,
    s_recv,
):
    rows = x_ref.shape[0]
    width, chans = lhs_ref.shape
    residues = x_ref.shape[1] // chans
    resid = residues // n
    tiles = x_ref.shape[1] // LANES
    per_tile = LANES // chans
    team = n // 2
    across = team // 4
    me = lax.axis_index("res")
    half = me // team
    seat = lax.rem(me, team)
    core = lax.rem(seat, 2)
    y = lax.rem(seat // 2, 2)
    z = seat // 4
    base = half * team
    partner = (1 - half) * team + seat
    peer_seat = seat + 1 - 2 * core

    def to(dev):
        return dict(device_id={"res": dev}, device_id_type=pl.DeviceIdType.MESH)

    def seat_at(z_step, flip, c):
        return lax.rem(z + z_step + across, across) * 4 + (1 - y if flip else y) * 2 + c

    barrier = pltpu.get_barrier_semaphore()

    def over(first, last, act):
        def step(k, carry):
            act(k)
            return carry

        lax.fori_loop(first, last, step, 0)

    def in_fours(count, act):
        step = 4 if count % 4 == 0 else 1

        def some(b):
            for u in range(step):
                act(b * step + u)

        over(0, count // step, some)

    over(1, team, lambda k: pl.semaphore_signal(barrier, inc=1, **to(base + lax.rem(seat + k, team))))
    pl.semaphore_signal(barrier, inc=1, **to(partner))

    def load(k, source, target):
        copy = pltpu.make_async_copy(source, target, in_sem.at[k])
        copy.start()
        return copy

    def x_half(which):
        wide = x_ref.shape[1] // 2
        at = pl.ds(pl.multiple_of((half if which else 1 - half) * wide, LANES), wide)
        return x_hbm.at[:, at], x_ref.at[:, at]

    small = [
        load(0, gain_hbm, gain_ref),
        load(1, offset_hbm, offset_ref),
        load(2, lhs_hbm, lhs_ref),
        load(3, rhs_hbm, rhs_ref),
    ]
    x_in = [load(4, *x_half(0)), load(5, *x_half(1))]
    pair_in = load(6, pair_hbm, pair_ref)
    for copy in small:
        copy.wait()

    def same(shape, down, across):
        r = lax.broadcasted_iota(jnp.int32, shape, 0) // down
        c = lax.broadcasted_iota(jnp.int32, shape, 1) // across
        return r == c

    reps = LANES // width
    lhs = jnp.concatenate([lhs_ref[...].astype(F32)] * per_tile, axis=1)
    lhs = jnp.concatenate([lhs] * reps, axis=0).T
    lhs_wide = jnp.concatenate([lhs] * (reps // per_tile), axis=0)
    lhs_wide = jnp.where(same(lhs_wide.shape, chans, width), lhs_wide, 0.0).astype(BF16)
    fold = width // WAVES
    rhs = rhs_ref[...].astype(F32)
    rhs_t = jnp.concatenate(
        [
            jnp.concatenate([rhs[k * fold : (k + 1) * fold] for k in (2 * g, 2 * g + 1)], axis=1)
            for g in range(WAVES // 2)
        ],
        axis=0,
    ).astype(BF16)
    averager = jnp.where(same((LANES, LANES), chans, chans), 1.0 / chans, 0.0).astype(BF16)
    gain = jnp.concatenate([gain_ref[...]] * per_tile, axis=1)
    offset = jnp.concatenate([offset_ref[...]] * per_tile, axis=1)

    group = 8
    dests = group * per_tile // resid
    halves = resid * width // LANES
    groups = tiles // 2 // group

    def project(b, which):
        start = ((half if which else 1 - half) * groups + b) * group
        x = jnp.concatenate(
            [
                x_ref[:, pl.ds(pl.multiple_of((start + u) * LANES, LANES), LANES)].astype(F32)
                for u in range(group)
            ],
            axis=0,
        )
        center = x - dot(x.astype(BF16), averager)
        square = center * center
        high = square.astype(BF16)
        low = (square - high.astype(F32)).astype(BF16)
        spread = dot(high, averager) + dot(low, averager)
        normed = (center * lax.rsqrt(spread + 1e-05) * gain + offset).astype(BF16)
        wide = normed.astype(F32)
        at = (which * groups + b) * group * rows
        norm_scr[pl.ds(pl.multiple_of(at, 8), group * rows), :] = wide
        even = jnp.concatenate(
            [wide[u * rows : (u + 1) * rows] for u in range(0, group, 2)], axis=0
        ).astype(BF16)
        odd = jnp.concatenate(
            [wide[u * rows : (u + 1) * rows] for u in range(1, group, 2)], axis=0
        ).astype(BF16)
        left = dot(jnp.concatenate([even, odd], axis=1), lhs_wide)
        for u in range(group // 2):
            left_send[
                which, b * dests + u // halves, :, (u % halves) * LANES : (u % halves + 1) * LANES
            ] = left[u * rows : (u + 1) * rows].astype(BF16)

    def left_copy(k, which, incoming):
        slot = team - k if incoming else k
        other = lax.rem(seat + k, team)
        return pltpu.make_async_remote_copy(
            src_ref=left_send.at[which, other],
            dst_ref=left_all.at[which, other if incoming else seat],
            send_sem=l_send.at[which, slot],
            recv_sem=l_recv.at[which, slot],
            **to(base + other),
        )

    part = fold * residues
    cut = part // LANES * BY_Y // 8 * LANES

    def own(w, k, incoming):
        z_step = 0 if isinstance(k, int) else (-k if incoming else k)
        flip = isinstance(k, int)
        other = seat_at(z_step, flip, core)
        ref = right_all.at[w, other if incoming else seat]
        return pltpu.make_async_remote_copy(
            src_ref=ref,
            dst_ref=ref,
            send_sem=own_send.at[w, k],
            recv_sem=own_recv.at[w, k],
            **to(base + other),
        )

    def relay_y(w, k, incoming):
        source = seat_at(-k, incoming, core)
        ref = right_all.at[w, source, :, pl.ds(0, cut)]
        return pltpu.make_async_remote_copy(
            src_ref=ref,
            dst_ref=ref,
            send_sem=y_send.at[w, k],
            recv_sem=y_recv.at[w, k],
            **to(base + seat_at(0, True, core)),
        )

    def relay_z(w, k, incoming):
        source = seat_at(-k if incoming else 0, True, core)
        ref = right_all.at[w, source, :, pl.ds(cut, part - cut)]
        return pltpu.make_async_remote_copy(
            src_ref=ref,
            dst_ref=ref,
            send_sem=z_send.at[w, k],
            recv_sem=z_recv.at[w, k],
            **to(base + seat_at(-k if incoming else k, False, core)),
        )

    def far(w, k, incoming):
        other = seat_at(-k if incoming else k, True, core)
        ref = right_all.at[w, other if incoming else seat]
        return pltpu.make_async_remote_copy(
            src_ref=ref,
            dst_ref=ref,
            send_sem=z_send.at[w, k],
            recv_sem=z_recv.at[w, k],
            **to(base + other),
        )

    def share(w, k, kind, incoming):
        source = seat_at(-k, kind > 0, 1 - core if incoming else core)
        ref = right_all.at[w, source]
        if kind == 1 and w >= DIRECT:
            ref = right_all.at[w, source, :, pl.ds(0, cut)]
        if kind == 2:
            ref = right_all.at[w, source, :, pl.ds(cut, part - cut)]
        return pltpu.make_async_remote_copy(
            src_ref=ref,
            dst_ref=ref,
            send_sem=peer_send.at[w, kind, k],
            recv_sem=peer_recv.at[w, kind, k],
            **to(base + peer_seat),
        )

    def share_near(w, incoming):
        source = seat_at(0, True, 1 - core if incoming else core)
        ref = right_all.at[w, source]
        return pltpu.make_async_remote_copy(
            src_ref=ref,
            dst_ref=ref,
            send_sem=peer_send.at[w, 1, 0],
            recv_sem=peer_recv.at[w, 1, 0],
            **to(base + peer_seat),
        )

    lane = lax.broadcasted_iota(jnp.int32, (tiles // WAVES, LANES), 1) // chans
    strips = residues // LANES
    wave_tiles = tiles // WAVES
    span = residues // WAVES
    batch = 8
    fold_lane = lax.broadcasted_iota(jnp.int32, (fold, LANES), 1) // (LANES // 2)

    def turn(b, w):
        ones = [
            norm_scr[pl.ds(w * wave_tiles * rows + b * batch + v, wave_tiles, stride=rows), :]
            for v in range(batch)
        ]
        picked = []
        for one in ones:
            rolled = pltpu.roll(one, chans, 1)
            picked += [jnp.where(lane == q, one if q == h else rolled, 0.0) for q in range(2) for h in range(2)]
        spread_out = jnp.concatenate(picked, axis=0).astype(BF16)
        res = lax.dot_general(
            rhs_t, spread_out, (((1,), (1,)), ((), ())), preferred_element_type=F32
        )
        deep = residues // 2

        def put(v, j, value):
            turn_scr[w * strips + j, pl.ds(b * batch + v, fold, stride=rows), :] = value

        if deep % LANES:
            for v in range(0, batch, 2):
                low = res[:fold, v * deep : v * deep + LANES]
                high = res[fold:, v * deep : v * deep + LANES]
                put(v, 0, jnp.where(fold_lane == 0, low, pltpu.roll(high, LANES // 2, 1)))
                put(v + 1, 0, jnp.where(fold_lane == 0, pltpu.roll(low, LANES // 2, 1), high))
        else:
            for v in range(batch):
                for j in range(strips):
                    g, at = j * LANES // deep, v * deep + j * LANES % deep
                    put(v, j, res[g * fold : (g + 1) * fold, at : at + LANES])

    def turned(w):
        in_fours(rows // batch, lambda b: turn(b, w))
        for q in range(fold):
            for j in range(strips):
                at = q * residues + j * LANES
                right_all[w, seat, :, at : at + LANES] = turn_scr[
                    w * strips + j, q * rows : (q + 1) * rows, :
                ].astype(BF16)

    def give(w):
        own(w, 0, False).start()
        over(1, across, lambda k: own(w, k, False).start())
        share(w, 0, 0, False).start()
        if w < DIRECT:
            over(1, across, lambda k: far(w, k, False).start())

    def relay(w):
        def along(k):
            own(w, k, True).wait_recv()
            if w >= DIRECT:
                relay_y(w, k, False).start()
            share(w, k, 0, False).start()

        own(w, 0, True).wait_recv()
        if w >= DIRECT:
            over(1, across, lambda k: relay_z(w, k, False).start())
        share_near(w, False).start()
        over(1, across, along)

    def pass_on(w):
        def along(k):
            if w < DIRECT:
                far(w, k, True).wait_recv()
                share(w, k, 1, False).start()
                return
            relay_y(w, k, True).wait_recv()
            share(w, k, 1, False).start()
            relay_z(w, k, True).wait_recv()
            share(w, k, 2, False).start()

        over(1, across, along)

    def gathered(w):
        over(0, across, lambda k: share(w, k, 0, True).wait_recv())
        share_near(w, True).wait_recv()

        def along(k):
            share(w, k, 1, True).wait_recv()
            if w >= DIRECT:
                share(w, k, 2, True).wait_recv()

        over(1, across, along)

    out_chans = pair_ref.shape[1]

    def prepare():
        pair_in.wait()
        pair_scr[...] = pair_ref[...].astype(F32)
        for c in range(WAVES):
            for b in range(fold // reps):
                some = jnp.concatenate(
                    [
                        pair_scr[pl.ds(c * fold + b * reps + u, width, stride=width), :]
                        for u in range(reps)
                    ],
                    axis=0,
                )
                pair_t[c * out_chans : (c + 1) * out_chans, b * LANES : (b + 1) * LANES] = (
                    some.T.astype(BF16)
                )

    qs = 4
    here_rows = team * rows
    total = n * rows
    slot = lax.broadcasted_iota(jnp.int32, (out_chans, residues), 1) // span

    def fill(which, w):
        for b in range(fold // qs):
            here = right_all[w, :, :, b * qs * residues : (b + 1) * qs * residues]
            if rows % 16:
                here = here.astype(F32)
            here = here.reshape(here_rows, qs * residues).astype(BF16)
            product = (dot(left_t[which], here) * (1.0 / total)).astype(BF16)
            for u in range(qs):
                for i in range(resid):
                    flat[
                        (b * qs + u) * width : (b * qs + u + 1) * width,
                        i * residues : (i + 1) * residues,
                    ] = product[i * width : (i + 1) * width, u * residues : (u + 1) * residues]

    def sums(b, w):
        return pltpu.make_async_remote_copy(
            src_ref=sum_send.at[w, b],
            dst_ref=sum_recv.at[w, b],
            send_sem=s_send.at[w, b],
            recv_sem=s_recv.at[w, b],
            **to(partner),
        )

    def mapped(b):
        both = dot(
            pair_t[...], flat[:, b * WAVES * residues : (b + 1) * WAVES * residues]
        )
        whole = None
        for d in range(WAVES):
            one = None
            for q in range(WAVES):
                i = (q + d) % WAVES
                piece = both[q * out_chans : (q + 1) * out_chans, i * residues : (i + 1) * residues]
                one = piece if one is None else jnp.where(slot == q, piece, one)
            if d:
                one = pltpu.roll(one, d * span, 1)
            whole = one if whole is None else whole + one
        return whole

    blocks = resid // WAVES

    def theirs(w):
        fill(0, w)
        for b in range(blocks):
            sum_send[w, b] = mapped(b).astype(BF16)
            sums(b, w).start()

    def mine(w):
        fill(1, w)
        for b in range(blocks):
            kept[w, b] = mapped(b)

    def finish(r):
        w = (r + WAVES // 2) % WAVES
        first = (half if 2 * w >= WAVES else 1 - half) * (residues // 2) + w % (WAVES // 2) * span
        for b in range(blocks):
            sums(b, r).wait_recv()
            done = (kept[w, b] + sum_recv[r, b].astype(F32)).T
            for u in range(WAVES):
                for h in range(2):
                    at = u * span + h * wave_tiles
                    out_ref[WAVES * b + u, pl.ds(first + h, wave_tiles, stride=2), :] = done[
                        at : at + wave_tiles
                    ]

    def left_turn(which):
        over(1, team, lambda k: left_copy(k, which, True).wait_recv())
        left_t[which] = (
            left_all[which].astype(F32).reshape(team * rows, resid * width).T.astype(BF16)
        )

    def left_give(which):
        over(1, team, lambda k: left_copy(k, which, False).start())
        left_all[which, seat] = left_send[which, seat]

    x_in[0].wait()
    in_fours(groups, lambda b: project(b, 0))
    pl.semaphore_wait(barrier, team)
    left_give(0)
    turned(0)
    give(0)
    turned(1)
    give(1)
    x_in[1].wait()
    in_fours(groups, lambda b: project(b, 1))
    relay(0)
    turned(2)
    give(2)
    relay(1)
    turned(3)
    give(3)
    pass_on(0)
    prepare()
    left_turn(0)
    gathered(0)
    theirs(0)
    relay(2)
    pass_on(1)
    gathered(1)
    theirs(1)
    relay(3)
    left_give(1)
    pass_on(2)
    gathered(2)
    theirs(2)
    pass_on(3)
    gathered(3)
    theirs(3)
    left_turn(1)
    mine(0)
    mine(1)
    mine(2)
    finish(0)
    mine(3)
    finish(1)
    finish(2)
    finish(3)

    for w in range(WAVES):
        own(w, 0, False).wait_send()
        over(1, across, lambda k: own(w, k, False).wait_send())
        if w < DIRECT:
            over(1, across, lambda k: far(w, k, False).wait_send())
        else:
            over(1, across, lambda k: relay_y(w, k, False).wait_send())
            over(1, across, lambda k: relay_z(w, k, False).wait_send())
        over(0, across, lambda k: share(w, k, 0, False).wait_send())
        share_near(w, False).wait_send()
        over(1, across, lambda k: share(w, k, 1, False).wait_send())
        if w >= DIRECT:
            over(1, across, lambda k: share(w, k, 2, False).wait_send())
        for b in range(blocks):
            sums(b, w).wait_send()
    for which in range(2):
        over(1, team, lambda k: left_copy(k, which, False).wait_send())


def on_device(n, x, gain, offset, lhs, rhs, pair, shift):
    rows = x.shape[0]
    chans, width = lhs.shape
    residues = x.shape[1] // chans
    resid = residues // n
    tiles = x.shape[1] // LANES
    team = n // 2
    across = team // 4
    depth = width * width
    out_chans = pair.shape[1]
    blocks = resid // WAVES
    fold = width // WAVES
    vmem = pl.BlockSpec(memory_space=pltpu.VMEM)
    args = [
        pltpu.with_memory_space_constraint(v, pltpu.HBM)
        for v in (x, gain.reshape(1, -1), offset.reshape(1, -1), lhs.T, rhs.T, pair)
    ]
    out = pl.pallas_call(
        functools.partial(kernel, n),
        out_shape=pltpu.VMEM((resid, residues, out_chans), F32),
        in_specs=[pl.BlockSpec(memory_space=pltpu.HBM)] * 6,
        out_specs=vmem,
        scratch_shapes=[
            pltpu.VMEM(x.shape, BF16),
            pltpu.VMEM((1, chans), F32),
            pltpu.VMEM((1, chans), F32),
            pltpu.VMEM((width, chans), BF16),
            pltpu.VMEM((width, chans), BF16),
            pltpu.VMEM(pair.shape, BF16),
            pltpu.SemaphoreType.DMA((7,)),
            pltpu.VMEM((tiles * rows, LANES), F32),
            pltpu.VMEM((WAVES * residues // LANES, fold * rows, LANES), F32),
            pltpu.VMEM((depth, out_chans), F32),
            pltpu.VMEM((WAVES * out_chans, depth // WAVES), BF16),
            pltpu.VMEM((2, team, rows, resid * width), BF16),
            pltpu.VMEM((2, team, rows, resid * width), BF16),
            pltpu.VMEM((2, resid * width, team * rows), BF16),
            pltpu.VMEM((WAVES, team, rows, fold * residues), BF16),
            pltpu.VMEM((depth // WAVES, resid * residues), BF16),
            pltpu.VMEM((WAVES, blocks, out_chans, residues), F32),
            pltpu.VMEM((WAVES, blocks, out_chans, residues), BF16),
            pltpu.VMEM((WAVES, blocks, out_chans, residues), BF16),
            pltpu.SemaphoreType.DMA((2, team)),
            pltpu.SemaphoreType.DMA((2, team)),
            pltpu.SemaphoreType.DMA((WAVES, across)),
            pltpu.SemaphoreType.DMA((WAVES, across)),
            pltpu.SemaphoreType.DMA((WAVES, across)),
            pltpu.SemaphoreType.DMA((WAVES, across)),
            pltpu.SemaphoreType.DMA((WAVES, across)),
            pltpu.SemaphoreType.DMA((WAVES, across)),
            pltpu.SemaphoreType.DMA((WAVES, 3, across)),
            pltpu.SemaphoreType.DMA((WAVES, 3, across)),
            pltpu.SemaphoreType.DMA((WAVES, blocks)),
            pltpu.SemaphoreType.DMA((WAVES, blocks)),
        ],
        compiler_params=pltpu.CompilerParams(
            collective_id=0, has_side_effects=True, vmem_limit_bytes=40 * 1024 * 1024
        ),
    )(*args)
    return (out + shift).astype(BF16)


def solution(mesh):
    in_specs = (P(("grp", "res"), None), P(), P(), P(), P(), P(), P())
    out_specs = P(("grp", "res"), None, None)
    return jax.shard_map(
        functools.partial(on_device, mesh.shape["res"]),
        mesh=mesh,
        in_specs=in_specs,
        out_specs=out_specs,
        check_vma=False,
    )
```

```python
import functools

import jax
import jax.numpy as jnp
from jax import lax
from jax.experimental import pallas as pl
from jax.experimental.pallas import tpu as pltpu
from jax.sharding import PartitionSpec as P

F32 = jnp.float32
BF16 = jnp.bfloat16
LANES = 128
WAVES = 4
BY_Y = 7
DIRECT = 1


def dot(a, b):
    return jnp.dot(a, b, preferred_element_type=F32)


def kernel(
    n,
    x_hbm,
    gain_hbm,
    offset_hbm,
    lhs_hbm,
    rhs_hbm,
    pair_hbm,
    out_ref,
    x_ref,
    gain_ref,
    offset_ref,
    lhs_ref,
    rhs_ref,
    pair_ref,
    in_sem,
    norm_scr,
    turn_scr,
    pair_scr,
    pair_t,
    left_send,
    left_all,
    left_t,
    right_all,
    flat,
    kept,
    sum_send,
    sum_recv,
    l_send,
    l_recv,
    own_send,
    own_recv,
    y_send,
    y_recv,
    z_send,
    z_recv,
    peer_send,
    peer_recv,
    s_send,
    s_recv,
):
    rows = x_ref.shape[0]
    width, chans = lhs_ref.shape
    residues = x_ref.shape[1] // chans
    resid = residues // n
    tiles = x_ref.shape[1] // LANES
    per_tile = LANES // chans
    team = n // 2
    across = team // 4
    me = lax.axis_index("res")
    half = me // team
    seat = lax.rem(me, team)
    core = lax.rem(seat, 2)
    y = lax.rem(seat // 2, 2)
    z = seat // 4
    base = half * team
    partner = (1 - half) * team + seat
    peer_seat = seat + 1 - 2 * core
    late = jnp.logical_and(half == 1, 2 * z >= across)

    def to(dev):
        return dict(device_id={"res": dev}, device_id_type=pl.DeviceIdType.MESH)

    def seat_at(z_step, flip, c):
        return lax.rem(z + z_step + across, across) * 4 + (1 - y if flip else y) * 2 + c

    barrier = pltpu.get_barrier_semaphore()

    def over(first, last, act):
        def step(k, carry):
            act(k)
            return carry

        lax.fori_loop(first, last, step, 0)

    def in_fours(count, act):
        step = max(k for k in (1, 2, 4) if count % k == 0)

        def some(b):
            for u in range(step):
                act(b * step + u)

        over(0, count // step, some)

    over(1, team, lambda k: pl.semaphore_signal(barrier, inc=1, **to(base + lax.rem(seat + k, team))))
    pl.semaphore_signal(barrier, inc=1, **to(partner))

    def load(k, source, target):
        copy = pltpu.make_async_copy(source, target, in_sem.at[k])
        copy.start()
        return copy

    def x_part(w):
        wide = x_ref.shape[1] // WAVES
        side = half if 2 * w >= WAVES else 1 - half
        at = pl.multiple_of((side * (WAVES // 2) + w % (WAVES // 2)) * wide, LANES)
        return x_hbm.at[:, pl.ds(at, wide)], x_ref.at[:, pl.ds(at, wide)]

    x_in = [load(4, *x_part(0))]
    small = [
        load(0, gain_hbm, gain_ref),
        load(1, offset_hbm, offset_ref),
        load(2, lhs_hbm, lhs_ref),
        load(3, rhs_hbm, rhs_ref),
    ]
    x_in += [load(4 + w, *x_part(w)) for w in range(1, WAVES)]
    pair_in = load(4 + WAVES, pair_hbm, pair_ref)
    for copy in small:
        copy.wait()

    def same(shape, down, across):
        r = lax.broadcasted_iota(jnp.int32, shape, 0) // down
        c = lax.broadcasted_iota(jnp.int32, shape, 1) // across
        return r == c

    reps = LANES // width
    lhs = jnp.concatenate([lhs_ref[...].astype(F32)] * per_tile, axis=1)
    lhs = jnp.concatenate([lhs] * reps, axis=0).T
    lhs_wide = jnp.concatenate([lhs] * (reps // per_tile), axis=0)
    lhs_wide = jnp.where(same(lhs_wide.shape, chans, width), lhs_wide, 0.0).astype(BF16)
    fold = width // WAVES
    rhs = rhs_ref[...].astype(F32)
    rhs_t = jnp.concatenate(
        [
            jnp.concatenate([rhs[k * fold : (k + 1) * fold] for k in (2 * g, 2 * g + 1)], axis=1)
            for g in range(WAVES // 2)
        ],
        axis=0,
    ).astype(BF16)
    averager = jnp.where(same((LANES, LANES), chans, chans), 1.0 / chans, 0.0).astype(BF16)
    gain = jnp.concatenate([gain_ref[...]] * per_tile, axis=1)
    offset = jnp.concatenate([offset_ref[...]] * per_tile, axis=1)

    group = 8
    dests = group * per_tile // resid
    halves = resid * width // LANES
    groups = tiles // 2 // group

    def project(b, which):
        start = ((half if which else 1 - half) * groups + b) * group
        x = jnp.concatenate(
            [
                x_ref[:, pl.ds(pl.multiple_of((start + u) * LANES, LANES), LANES)].astype(F32)
                for u in range(group)
            ],
            axis=0,
        )
        center = x - dot(x.astype(BF16), averager)
        square = center * center
        high = square.astype(BF16)
        low = (square - high.astype(F32)).astype(BF16)
        spread = dot(high, averager) + dot(low, averager)
        normed = (center * lax.rsqrt(spread + 1e-05) * gain + offset).astype(BF16)
        wide = normed.astype(F32)
        at = (which * groups + b) * group * rows
        norm_scr[pl.ds(pl.multiple_of(at, 8), group * rows), :] = wide
        even = jnp.concatenate(
            [wide[u * rows : (u + 1) * rows] for u in range(0, group, 2)], axis=0
        ).astype(BF16)
        odd = jnp.concatenate(
            [wide[u * rows : (u + 1) * rows] for u in range(1, group, 2)], axis=0
        ).astype(BF16)
        left = dot(jnp.concatenate([even, odd], axis=1), lhs_wide)
        for u in range(group // 2):
            left_send[
                which, b * dests + u // halves, :, (u % halves) * LANES : (u % halves + 1) * LANES
            ] = left[u * rows : (u + 1) * rows].astype(BF16)

    def projected(w):
        x_in[w].wait()
        count = groups // (WAVES // 2)
        in_fours(count, lambda b: project(w % (WAVES // 2) * count + b, w // (WAVES // 2)))

    def left_copy(k, which, incoming):
        slot = team - k if incoming else k
        other = lax.rem(seat + k, team)
        return pltpu.make_async_remote_copy(
            src_ref=left_send.at[which, other],
            dst_ref=left_all.at[which, other if incoming else seat],
            send_sem=l_send.at[which, slot],
            recv_sem=l_recv.at[which, slot],
            **to(base + other),
        )

    part = fold * residues
    cut = part // LANES * BY_Y // 8 * LANES

    def own(w, k, incoming):
        z_step = 0 if isinstance(k, int) else (-k if incoming else k)
        flip = isinstance(k, int)
        other = seat_at(z_step, flip, core)
        ref = right_all.at[w, other if incoming else seat]
        return pltpu.make_async_remote_copy(
            src_ref=ref,
            dst_ref=ref,
            send_sem=own_send.at[w, k],
            recv_sem=own_recv.at[w, k],
            **to(base + other),
        )

    def relay_y(w, k, incoming):
        source = seat_at(-k, incoming, core)
        ref = right_all.at[w, source, :, pl.ds(0, cut)]
        return pltpu.make_async_remote_copy(
            src_ref=ref,
            dst_ref=ref,
            send_sem=y_send.at[w, k],
            recv_sem=y_recv.at[w, k],
            **to(base + seat_at(0, True, core)),
        )

    def relay_z(w, k, incoming):
        source = seat_at(-k if incoming else 0, True, core)
        ref = right_all.at[w, source, :, pl.ds(cut, part - cut)]
        return pltpu.make_async_remote_copy(
            src_ref=ref,
            dst_ref=ref,
            send_sem=z_send.at[w, k],
            recv_sem=z_recv.at[w, k],
            **to(base + seat_at(-k if incoming else k, False, core)),
        )

    def far(w, k, incoming):
        other = seat_at(-k if incoming else k, True, core)
        ref = right_all.at[w, other if incoming else seat]
        return pltpu.make_async_remote_copy(
            src_ref=ref,
            dst_ref=ref,
            send_sem=z_send.at[w, k],
            recv_sem=z_recv.at[w, k],
            **to(base + other),
        )

    def share(w, k, kind, incoming):
        source = seat_at(-k, kind > 0, 1 - core if incoming else core)
        ref = right_all.at[w, source]
        if kind == 1 and w >= DIRECT:
            ref = right_all.at[w, source, :, pl.ds(0, cut)]
        if kind == 2:
            ref = right_all.at[w, source, :, pl.ds(cut, part - cut)]
        return pltpu.make_async_remote_copy(
            src_ref=ref,
            dst_ref=ref,
            send_sem=peer_send.at[w, kind, k],
            recv_sem=peer_recv.at[w, kind, k],
            **to(base + peer_seat),
        )

    def share_near(w, incoming):
        source = seat_at(0, True, 1 - core if incoming else core)
        ref = right_all.at[w, source]
        return pltpu.make_async_remote_copy(
            src_ref=ref,
            dst_ref=ref,
            send_sem=peer_send.at[w, 1, 0],
            recv_sem=peer_recv.at[w, 1, 0],
            **to(base + peer_seat),
        )

    lane = lax.broadcasted_iota(jnp.int32, (tiles // WAVES, LANES), 1) // chans
    strips = residues // LANES
    wave_tiles = tiles // WAVES
    span = residues // WAVES
    batch = 8
    fold_lane = lax.broadcasted_iota(jnp.int32, (fold, LANES), 1) // (LANES // 2)

    def turn(b, w):
        ones = [
            norm_scr[pl.ds(w * wave_tiles * rows + b * batch + v, wave_tiles, stride=rows), :]
            for v in range(batch)
        ]
        picked = []
        for one in ones:
            rolled = pltpu.roll(one, chans, 1)
            picked += [jnp.where(lane == q, one if q == h else rolled, 0.0) for q in range(2) for h in range(2)]
        spread_out = jnp.concatenate(picked, axis=0).astype(BF16)
        res = lax.dot_general(
            rhs_t, spread_out, (((1,), (1,)), ((), ())), preferred_element_type=F32
        )
        deep = residues // 2

        def put(v, j, value):
            turn_scr[w * strips + j, pl.ds(b * batch + v, fold, stride=rows), :] = value

        if deep % LANES:
            for v in range(0, batch, 2):
                low = res[:fold, v * deep : v * deep + LANES]
                high = res[fold:, v * deep : v * deep + LANES]
                put(v, 0, jnp.where(fold_lane == 0, low, pltpu.roll(high, LANES // 2, 1)))
                put(v + 1, 0, jnp.where(fold_lane == 0, pltpu.roll(low, LANES // 2, 1), high))
        else:
            for v in range(batch):
                for j in range(strips):
                    g, at = j * LANES // deep, v * deep + j * LANES % deep
                    put(v, j, res[g * fold : (g + 1) * fold, at : at + LANES])

    def turned(w):
        in_fours(rows // batch, lambda b: turn(b, w))
        for q in range(fold):
            for j in range(strips):
                at = q * residues + j * LANES
                right_all[w, seat, :, at : at + LANES] = turn_scr[
                    w * strips + j, q * rows : (q + 1) * rows, :
                ].astype(BF16)

    def give(w):
        own(w, 0, False).start()
        over(1, across, lambda k: own(w, k, False).start())
        share(w, 0, 0, False).start()
        if w < DIRECT:
            over(1, across, lambda k: far(w, k, False).start())

    def relay(w):
        def along(k):
            own(w, k, True).wait_recv()
            if w >= DIRECT:
                relay_y(w, k, False).start()
            share(w, k, 0, False).start()

        own(w, 0, True).wait_recv()
        if w >= DIRECT:
            over(1, across, lambda k: relay_z(w, k, False).start())
        share_near(w, False).start()
        over(1, across, along)

    def pass_on(w):
        def along(k):
            if w < DIRECT:
                far(w, k, True).wait_recv()
                share(w, k, 1, False).start()
                return
            relay_y(w, k, True).wait_recv()
            share(w, k, 1, False).start()
            relay_z(w, k, True).wait_recv()
            share(w, k, 2, False).start()

        over(1, across, along)

    def gathered(w):
        over(0, across, lambda k: share(w, k, 0, True).wait_recv())
        share_near(w, True).wait_recv()

        def along(k):
            share(w, k, 1, True).wait_recv()
            if w >= DIRECT:
                share(w, k, 2, True).wait_recv()

        over(1, across, along)

    out_chans = pair_ref.shape[1]

    def prepare():
        pair_in.wait()
        pair_scr[...] = pair_ref[...].astype(F32)
        for c in range(WAVES):
            for b in range(fold // reps):
                some = jnp.concatenate(
                    [
                        pair_scr[pl.ds(c * fold + b * reps + u, width, stride=width), :]
                        for u in range(reps)
                    ],
                    axis=0,
                )
                pair_t[c * out_chans : (c + 1) * out_chans, b * LANES : (b + 1) * LANES] = (
                    some.T.astype(BF16)
                )

    qs = 4
    here_rows = team * rows
    total = n * rows
    slot = lax.broadcasted_iota(jnp.int32, (out_chans, residues), 1) // span

    def fill(which, w):
        for b in range(fold // qs):
            here = right_all[w, :, :, b * qs * residues : (b + 1) * qs * residues]
            if rows % 16:
                here = here.astype(F32)
            here = here.reshape(here_rows, qs * residues).astype(BF16)
            product = (dot(left_t[which], here) * (1.0 / total)).astype(BF16)
            for u in range(qs):
                for i in range(resid):
                    flat[
                        (b * qs + u) * width : (b * qs + u + 1) * width,
                        i * residues : (i + 1) * residues,
                    ] = product[i * width : (i + 1) * width, u * residues : (u + 1) * residues]

    def sums(b, w):
        return pltpu.make_async_remote_copy(
            src_ref=sum_send.at[w, b],
            dst_ref=sum_recv.at[w, b],
            send_sem=s_send.at[w, b],
            recv_sem=s_recv.at[w, b],
            **to(partner),
        )

    def mapped(b):
        both = dot(
            pair_t[...], flat[:, b * WAVES * residues : (b + 1) * WAVES * residues]
        )
        whole = None
        for d in range(WAVES):
            one = None
            for q in range(WAVES):
                i = (q + d) % WAVES
                piece = both[q * out_chans : (q + 1) * out_chans, i * residues : (i + 1) * residues]
                one = piece if one is None else jnp.where(slot == q, piece, one)
            if d:
                one = pltpu.roll(one, d * span, 1)
            whole = one if whole is None else whole + one
        return whole

    blocks = resid // WAVES

    def theirs(w):
        fill(0, w)
        for b in range(blocks):
            sum_send[w, b] = mapped(b).astype(BF16)

            @pl.when(jnp.logical_not(late))
            def _():
                sums(b, w).start()

    def flush(w):
        @pl.when(late)
        def _():
            for b in range(blocks):
                sums(b, w).start()

    def mine(w):
        fill(1, w)
        for b in range(blocks):
            kept[w, b] = mapped(b)

    def finish(r):
        w = (r + WAVES // 2) % WAVES
        first = (half if 2 * w >= WAVES else 1 - half) * (residues // 2) + w % (WAVES // 2) * span
        for b in range(blocks):
            sums(b, r).wait_recv()
            done = (kept[w, b] + sum_recv[r, b].astype(F32)).T
            for u in range(WAVES):
                for h in range(2):
                    at = u * span + h * wave_tiles
                    out_ref[WAVES * b + u, pl.ds(first + h, wave_tiles, stride=2), :] = done[
                        at : at + wave_tiles
                    ]

    def left_turn(which):
        over(1, team, lambda k: left_copy(k, which, True).wait_recv())
        left_t[which] = (
            left_all[which].astype(F32).reshape(team * rows, resid * width).T.astype(BF16)
        )

    def left_give(which):
        over(1, team, lambda k: left_copy(k, which, False).start())
        left_all[which, seat] = left_send[which, seat]

    projected(0)
    turned(0)
    pl.semaphore_wait(barrier, team)
    give(0)
    projected(1)
    left_give(0)
    turned(1)
    give(1)
    projected(2)
    turned(2)
    relay(0)
    give(2)
    projected(3)
    turned(3)
    relay(1)
    give(3)
    pass_on(0)
    prepare()
    left_turn(0)
    gathered(0)
    theirs(0)
    flush(0)
    relay(2)
    pass_on(1)
    gathered(1)
    theirs(1)
    flush(1)
    relay(3)
    left_give(1)
    pass_on(2)
    gathered(2)
    theirs(2)
    flush(2)
    pass_on(3)
    gathered(3)
    theirs(3)
    flush(3)
    left_turn(1)
    mine(0)
    mine(1)
    mine(2)
    finish(0)
    mine(3)
    finish(1)
    finish(2)
    finish(3)

    for w in range(WAVES):
        own(w, 0, False).wait_send()
        over(1, across, lambda k: own(w, k, False).wait_send())
        if w < DIRECT:
            over(1, across, lambda k: far(w, k, False).wait_send())
        else:
            over(1, across, lambda k: relay_y(w, k, False).wait_send())
            over(1, across, lambda k: relay_z(w, k, False).wait_send())
        over(0, across, lambda k: share(w, k, 0, False).wait_send())
        share_near(w, False).wait_send()
        over(1, across, lambda k: share(w, k, 1, False).wait_send())
        if w >= DIRECT:
            over(1, across, lambda k: share(w, k, 2, False).wait_send())
        for b in range(blocks):
            sums(b, w).wait_send()
    for which in range(2):
        over(1, team, lambda k: left_copy(k, which, False).wait_send())


def on_device(n, x, gain, offset, lhs, rhs, pair, shift):
    rows = x.shape[0]
    chans, width = lhs.shape
    residues = x.shape[1] // chans
    resid = residues // n
    tiles = x.shape[1] // LANES
    team = n // 2
    across = team // 4
    depth = width * width
    out_chans = pair.shape[1]
    blocks = resid // WAVES
    fold = width // WAVES
    vmem = pl.BlockSpec(memory_space=pltpu.VMEM)
    args = [
        pltpu.with_memory_space_constraint(v, pltpu.HBM)
        for v in (x, gain.reshape(1, -1), offset.reshape(1, -1), lhs.T, rhs.T, pair)
    ]
    out = pl.pallas_call(
        functools.partial(kernel, n),
        out_shape=pltpu.VMEM((resid, residues, out_chans), F32),
        in_specs=[pl.BlockSpec(memory_space=pltpu.HBM)] * 6,
        out_specs=vmem,
        scratch_shapes=[
            pltpu.VMEM(x.shape, BF16),
            pltpu.VMEM((1, chans), F32),
            pltpu.VMEM((1, chans), F32),
            pltpu.VMEM((width, chans), BF16),
            pltpu.VMEM((width, chans), BF16),
            pltpu.VMEM(pair.shape, BF16),
            pltpu.SemaphoreType.DMA((5 + WAVES,)),
            pltpu.VMEM((tiles * rows, LANES), F32),
            pltpu.VMEM((WAVES * residues // LANES, fold * rows, LANES), F32),
            pltpu.VMEM((depth, out_chans), F32),
            pltpu.VMEM((WAVES * out_chans, depth // WAVES), BF16),
            pltpu.VMEM((2, team, rows, resid * width), BF16),
            pltpu.VMEM((2, team, rows, resid * width), BF16),
            pltpu.VMEM((2, resid * width, team * rows), BF16),
            pltpu.VMEM((WAVES, team, rows, fold * residues), BF16),
            pltpu.VMEM((depth // WAVES, resid * residues), BF16),
            pltpu.VMEM((WAVES, blocks, out_chans, residues), F32),
            pltpu.VMEM((WAVES, blocks, out_chans, residues), BF16),
            pltpu.VMEM((WAVES, blocks, out_chans, residues), BF16),
            pltpu.SemaphoreType.DMA((2, team)),
            pltpu.SemaphoreType.DMA((2, team)),
            pltpu.SemaphoreType.DMA((WAVES, across)),
            pltpu.SemaphoreType.DMA((WAVES, across)),
            pltpu.SemaphoreType.DMA((WAVES, across)),
            pltpu.SemaphoreType.DMA((WAVES, across)),
            pltpu.SemaphoreType.DMA((WAVES, across)),
            pltpu.SemaphoreType.DMA((WAVES, across)),
            pltpu.SemaphoreType.DMA((WAVES, 3, across)),
            pltpu.SemaphoreType.DMA((WAVES, 3, across)),
            pltpu.SemaphoreType.DMA((WAVES, blocks)),
            pltpu.SemaphoreType.DMA((WAVES, blocks)),
        ],
        compiler_params=pltpu.CompilerParams(
            collective_id=0, has_side_effects=True, vmem_limit_bytes=40 * 1024 * 1024
        ),
    )(*args)
    return (out + shift).astype(BF16)


def solution(mesh):
    in_specs = (P(("grp", "res"), None), P(), P(), P(), P(), P(), P())
    out_specs = P(("grp", "res"), None, None)
    return jax.shard_map(
        functools.partial(on_device, mesh.shape["res"]),
        mesh=mesh,
        in_specs=in_specs,
        out_specs=out_specs,
        check_vma=False,
    )
```

```python
import functools

import jax
import jax.numpy as jnp
from jax import lax
from jax.experimental import pallas as pl
from jax.experimental.pallas import tpu as pltpu
from jax.sharding import PartitionSpec as P

F32 = jnp.float32
BF16 = jnp.bfloat16
LANES = 128
WAVES = 4
BY_Y = 7
UNROLL = 8
DIRECT = 1


def dot(a, b):
    return jnp.dot(a, b, preferred_element_type=F32)


def kernel(
    n,
    x_hbm,
    gain_hbm,
    offset_hbm,
    lhs_hbm,
    rhs_hbm,
    pair_hbm,
    out_ref,
    x_ref,
    gain_ref,
    offset_ref,
    lhs_ref,
    rhs_ref,
    pair_ref,
    in_sem,
    norm_scr,
    turn_scr,
    pair_scr,
    pair_t,
    left_send,
    left_all,
    left_t,
    right_all,
    flat,
    kept,
    sum_send,
    sum_recv,
    l_send,
    l_recv,
    own_send,
    own_recv,
    y_send,
    y_recv,
    z_send,
    z_recv,
    peer_send,
    peer_recv,
    s_send,
    s_recv,
):
    rows = x_ref.shape[0]
    width, chans = lhs_ref.shape
    residues = x_ref.shape[1] // chans
    resid = residues // n
    tiles = x_ref.shape[1] // LANES
    per_tile = LANES // chans
    team = n // 2
    across = team // 4
    me = lax.axis_index("res")
    half = me // team
    seat = lax.rem(me, team)
    core = lax.rem(seat, 2)
    y = lax.rem(seat // 2, 2)
    z = seat // 4
    base = half * team
    partner = (1 - half) * team + seat
    peer_seat = seat + 1 - 2 * core
    late = jnp.logical_and(half == 1, 2 * z >= across)

    def to(dev):
        return dict(device_id={"res": dev}, device_id_type=pl.DeviceIdType.MESH)

    def seat_at(z_step, flip, c):
        return lax.rem(z + z_step + across, across) * 4 + (1 - y if flip else y) * 2 + c

    barrier = pltpu.get_barrier_semaphore()

    def over(first, last, act):
        if last - first <= UNROLL:
            for k in range(first, last):
                act(k)
            return

        def step(k, carry):
            act(k)
            return carry

        lax.fori_loop(first, last, step, 0)

    def in_fours(count, act):
        step = max(k for k in (1, 2, 4) if count % k == 0)

        def some(b):
            for u in range(step):
                act(b * step + u)

        over(0, count // step, some)

    over(1, team, lambda k: pl.semaphore_signal(barrier, inc=1, **to(base + lax.rem(seat + k, team))))
    pl.semaphore_signal(barrier, inc=1, **to(partner))

    def load(k, source, target):
        copy = pltpu.make_async_copy(source, target, in_sem.at[k])
        copy.start()
        return copy

    def x_part(w):
        wide = x_ref.shape[1] // WAVES
        side = half if 2 * w >= WAVES else 1 - half
        at = pl.multiple_of((side * (WAVES // 2) + w % (WAVES // 2)) * wide, LANES)
        return x_hbm.at[:, pl.ds(at, wide)], x_ref.at[:, pl.ds(at, wide)]

    x_in = [load(4, *x_part(0))]
    small = [
        load(0, gain_hbm, gain_ref),
        load(1, offset_hbm, offset_ref),
        load(2, lhs_hbm, lhs_ref),
        load(3, rhs_hbm, rhs_ref),
    ]
    x_in += [load(4 + w, *x_part(w)) for w in range(1, WAVES)]
    pair_in = load(4 + WAVES, pair_hbm, pair_ref)
    for copy in small:
        copy.wait()

    def same(shape, down, across):
        r = lax.broadcasted_iota(jnp.int32, shape, 0) // down
        c = lax.broadcasted_iota(jnp.int32, shape, 1) // across
        return r == c

    reps = LANES // width
    lhs = jnp.concatenate([lhs_ref[...].astype(F32)] * per_tile, axis=1)
    lhs = jnp.concatenate([lhs] * reps, axis=0).T
    lhs_wide = jnp.concatenate([lhs] * (reps // per_tile), axis=0)
    lhs_wide = jnp.where(same(lhs_wide.shape, chans, width), lhs_wide, 0.0).astype(BF16)
    fold = width // WAVES
    rhs = rhs_ref[...].astype(F32)
    rhs_t = jnp.concatenate(
        [
            jnp.concatenate([rhs[k * fold : (k + 1) * fold] for k in (2 * g, 2 * g + 1)], axis=1)
            for g in range(WAVES // 2)
        ],
        axis=0,
    ).astype(BF16)
    averager = jnp.where(same((LANES, LANES), chans, chans), 1.0 / chans, 0.0).astype(BF16)
    gain = jnp.concatenate([gain_ref[...]] * per_tile, axis=1)
    offset = jnp.concatenate([offset_ref[...]] * per_tile, axis=1)

    group = 8
    dests = group * per_tile // resid
    halves = resid * width // LANES
    groups = tiles // 2 // group

    def project(b, which):
        start = ((half if which else 1 - half) * groups + b) * group
        x = jnp.concatenate(
            [
                x_ref[:, pl.ds(pl.multiple_of((start + u) * LANES, LANES), LANES)].astype(F32)
                for u in range(group)
            ],
            axis=0,
        )
        center = x - dot(x.astype(BF16), averager)
        square = center * center
        high = square.astype(BF16)
        low = (square - high.astype(F32)).astype(BF16)
        spread = dot(high, averager) + dot(low, averager)
        normed = (center * lax.rsqrt(spread + 1e-05) * gain + offset).astype(BF16)
        wide = normed.astype(F32)
        at = (which * groups + b) * group * rows
        norm_scr[pl.ds(pl.multiple_of(at, 8), group * rows), :] = wide
        even = jnp.concatenate(
            [wide[u * rows : (u + 1) * rows] for u in range(0, group, 2)], axis=0
        ).astype(BF16)
        odd = jnp.concatenate(
            [wide[u * rows : (u + 1) * rows] for u in range(1, group, 2)], axis=0
        ).astype(BF16)
        left = dot(jnp.concatenate([even, odd], axis=1), lhs_wide)
        for u in range(group // 2):
            left_send[
                which, b * dests + u // halves, :, (u % halves) * LANES : (u % halves + 1) * LANES
            ] = left[u * rows : (u + 1) * rows].astype(BF16)

    def projected(w):
        x_in[w].wait()
        count = groups // (WAVES // 2)
        in_fours(count, lambda b: project(w % (WAVES // 2) * count + b, w // (WAVES // 2)))

    def left_copy(k, which, incoming):
        slot = team - k if incoming else k
        other = lax.rem(seat + k, team)
        return pltpu.make_async_remote_copy(
            src_ref=left_send.at[which, other],
            dst_ref=left_all.at[which, other if incoming else seat],
            send_sem=l_send.at[which, slot],
            recv_sem=l_recv.at[which, slot],
            **to(base + other),
        )

    part = fold * residues
    cut = part // LANES * BY_Y // 8 * LANES

    def own(w, k, incoming):
        flip = isinstance(k, int) and k == 0
        z_step = 0 if flip else (-k if incoming else k)
        other = seat_at(z_step, flip, core)
        ref = right_all.at[w, other if incoming else seat]
        return pltpu.make_async_remote_copy(
            src_ref=ref,
            dst_ref=ref,
            send_sem=own_send.at[w, k],
            recv_sem=own_recv.at[w, k],
            **to(base + other),
        )

    def relay_y(w, k, incoming):
        source = seat_at(-k, incoming, core)
        ref = right_all.at[w, source, :, pl.ds(0, cut)]
        return pltpu.make_async_remote_copy(
            src_ref=ref,
            dst_ref=ref,
            send_sem=y_send.at[w, k],
            recv_sem=y_recv.at[w, k],
            **to(base + seat_at(0, True, core)),
        )

    def relay_z(w, k, incoming):
        source = seat_at(-k if incoming else 0, True, core)
        ref = right_all.at[w, source, :, pl.ds(cut, part - cut)]
        return pltpu.make_async_remote_copy(
            src_ref=ref,
            dst_ref=ref,
            send_sem=z_send.at[w, k],
            recv_sem=z_recv.at[w, k],
            **to(base + seat_at(-k if incoming else k, False, core)),
        )

    def far(w, k, incoming):
        other = seat_at(-k if incoming else k, True, core)
        ref = right_all.at[w, other if incoming else seat]
        return pltpu.make_async_remote_copy(
            src_ref=ref,
            dst_ref=ref,
            send_sem=z_send.at[w, k],
            recv_sem=z_recv.at[w, k],
            **to(base + other),
        )

    def share(w, k, kind, incoming):
        source = seat_at(-k, kind > 0, 1 - core if incoming else core)
        ref = right_all.at[w, source]
        if kind == 1 and w >= DIRECT:
            ref = right_all.at[w, source, :, pl.ds(0, cut)]
        if kind == 2:
            ref = right_all.at[w, source, :, pl.ds(cut, part - cut)]
        return pltpu.make_async_remote_copy(
            src_ref=ref,
            dst_ref=ref,
            send_sem=peer_send.at[w, kind, k],
            recv_sem=peer_recv.at[w, kind, k],
            **to(base + peer_seat),
        )

    def share_near(w, incoming):
        source = seat_at(0, True, 1 - core if incoming else core)
        ref = right_all.at[w, source]
        return pltpu.make_async_remote_copy(
            src_ref=ref,
            dst_ref=ref,
            send_sem=peer_send.at[w, 1, 0],
            recv_sem=peer_recv.at[w, 1, 0],
            **to(base + peer_seat),
        )

    lane = lax.broadcasted_iota(jnp.int32, (tiles // WAVES, LANES), 1) // chans
    strips = residues // LANES
    wave_tiles = tiles // WAVES
    span = residues // WAVES
    batch = 8
    fold_lane = lax.broadcasted_iota(jnp.int32, (fold, LANES), 1) // (LANES // 2)

    def turn(b, w):
        ones = [
            norm_scr[pl.ds(w * wave_tiles * rows + b * batch + v, wave_tiles, stride=rows), :]
            for v in range(batch)
        ]
        picked = []
        for one in ones:
            rolled = pltpu.roll(one, chans, 1)
            picked += [jnp.where(lane == q, one if q == h else rolled, 0.0) for q in range(2) for h in range(2)]
        spread_out = jnp.concatenate(picked, axis=0).astype(BF16)
        res = lax.dot_general(
            rhs_t, spread_out, (((1,), (1,)), ((), ())), preferred_element_type=F32
        )
        deep = residues // 2

        def put(v, j, value):
            turn_scr[w * strips + j, pl.ds(b * batch + v, fold, stride=rows), :] = value

        if deep % LANES:
            for v in range(0, batch, 2):
                low = res[:fold, v * deep : v * deep + LANES]
                high = res[fold:, v * deep : v * deep + LANES]
                put(v, 0, jnp.where(fold_lane == 0, low, pltpu.roll(high, LANES // 2, 1)))
                put(v + 1, 0, jnp.where(fold_lane == 0, pltpu.roll(low, LANES // 2, 1), high))
        else:
            for v in range(batch):
                for j in range(strips):
                    g, at = j * LANES // deep, v * deep + j * LANES % deep
                    put(v, j, res[g * fold : (g + 1) * fold, at : at + LANES])

    def turned(w):
        in_fours(rows // batch, lambda b: turn(b, w))
        for q in range(fold):
            for j in range(strips):
                at = q * residues + j * LANES
                right_all[w, seat, :, at : at + LANES] = turn_scr[
                    w * strips + j, q * rows : (q + 1) * rows, :
                ].astype(BF16)

    def give(w):
        own(w, 0, False).start()
        over(1, across, lambda k: own(w, k, False).start())
        share(w, 0, 0, False).start()
        if w < DIRECT:
            over(1, across, lambda k: far(w, k, False).start())

    def relay(w):
        def along(k):
            own(w, k, True).wait_recv()
            if w >= DIRECT:
                relay_y(w, k, False).start()
            share(w, k, 0, False).start()

        own(w, 0, True).wait_recv()
        if w >= DIRECT:
            over(1, across, lambda k: relay_z(w, k, False).start())
        share_near(w, False).start()
        over(1, across, along)

    def pass_on(w):
        def along(k):
            if w < DIRECT:
                far(w, k, True).wait_recv()
                share(w, k, 1, False).start()
                return
            relay_y(w, k, True).wait_recv()
            share(w, k, 1, False).start()
            relay_z(w, k, True).wait_recv()
            share(w, k, 2, False).start()

        over(1, across, along)

    def gathered(w):
        over(0, across, lambda k: share(w, k, 0, True).wait_recv())
        share_near(w, True).wait_recv()

        def along(k):
            share(w, k, 1, True).wait_recv()
            if w >= DIRECT:
                share(w, k, 2, True).wait_recv()

        over(1, across, along)

    out_chans = pair_ref.shape[1]

    def prepare():
        pair_in.wait()
        pair_scr[...] = pair_ref[...].astype(F32)
        for c in range(WAVES):
            for b in range(fold // reps):
                some = jnp.concatenate(
                    [
                        pair_scr[pl.ds(c * fold + b * reps + u, width, stride=width), :]
                        for u in range(reps)
                    ],
                    axis=0,
                )
                pair_t[c * out_chans : (c + 1) * out_chans, b * LANES : (b + 1) * LANES] = (
                    some.T.astype(BF16)
                )

    qs = 4
    here_rows = team * rows
    total = n * rows
    slot = lax.broadcasted_iota(jnp.int32, (out_chans, residues), 1) // span

    def fill(which, w):
        for b in range(fold // qs):
            here = right_all[w, :, :, b * qs * residues : (b + 1) * qs * residues]
            if rows % 16:
                here = here.astype(F32)
            here = here.reshape(here_rows, qs * residues).astype(BF16)
            product = (dot(left_t[which], here) * (1.0 / total)).astype(BF16)
            for u in range(qs):
                for i in range(resid):
                    flat[
                        (b * qs + u) * width : (b * qs + u + 1) * width,
                        i * residues : (i + 1) * residues,
                    ] = product[i * width : (i + 1) * width, u * residues : (u + 1) * residues]

    def sums(b, w):
        return pltpu.make_async_remote_copy(
            src_ref=sum_send.at[w, b],
            dst_ref=sum_recv.at[w, b],
            send_sem=s_send.at[w, b],
            recv_sem=s_recv.at[w, b],
            **to(partner),
        )

    def mapped(b):
        both = dot(
            pair_t[...], flat[:, b * WAVES * residues : (b + 1) * WAVES * residues]
        )
        whole = None
        for d in range(WAVES):
            one = None
            for q in range(WAVES):
                i = (q + d) % WAVES
                piece = both[q * out_chans : (q + 1) * out_chans, i * residues : (i + 1) * residues]
                one = piece if one is None else jnp.where(slot == q, piece, one)
            if d:
                one = pltpu.roll(one, d * span, 1)
            whole = one if whole is None else whole + one
        return whole

    blocks = resid // WAVES

    def theirs(w):
        fill(0, w)
        for b in range(blocks):
            sum_send[w, b] = mapped(b).astype(BF16)

            @pl.when(jnp.logical_not(late))
            def _():
                sums(b, w).start()

    def flush(w):
        @pl.when(late)
        def _():
            for b in range(blocks):
                sums(b, w).start()

    def mine(w):
        fill(1, w)
        for b in range(blocks):
            kept[w, b] = mapped(b)

    def finish(r):
        w = (r + WAVES // 2) % WAVES
        first = (half if 2 * w >= WAVES else 1 - half) * (residues // 2) + w % (WAVES // 2) * span
        for b in range(blocks):
            sums(b, r).wait_recv()
            done = (kept[w, b] + sum_recv[r, b].astype(F32)).T
            for u in range(WAVES):
                for h in range(2):
                    at = u * span + h * wave_tiles
                    out_ref[WAVES * b + u, pl.ds(first + h, wave_tiles, stride=2), :] = done[
                        at : at + wave_tiles
                    ]

    def left_turn(which):
        over(1, team, lambda k: left_copy(k, which, True).wait_recv())
        left_t[which] = (
            left_all[which].astype(F32).reshape(team * rows, resid * width).T.astype(BF16)
        )

    def left_give(which):
        over(1, team, lambda k: left_copy(k, which, False).start())
        left_all[which, seat] = left_send[which, seat]

    def sent():
        for w in range(WAVES):
            own(w, 0, False).wait_send()
            over(1, across, lambda k: own(w, k, False).wait_send())
            if w < DIRECT:
                over(1, across, lambda k: far(w, k, False).wait_send())
            else:
                over(1, across, lambda k: relay_y(w, k, False).wait_send())
                over(1, across, lambda k: relay_z(w, k, False).wait_send())
            over(0, across, lambda k: share(w, k, 0, False).wait_send())
            share_near(w, False).wait_send()
            over(1, across, lambda k: share(w, k, 1, False).wait_send())
            if w >= DIRECT:
                over(1, across, lambda k: share(w, k, 2, False).wait_send())
        for which in range(2):
            over(1, team, lambda k: left_copy(k, which, False).wait_send())

    projected(0)
    turned(0)
    pl.semaphore_wait(barrier, team)
    give(0)
    projected(1)
    left_give(0)
    turned(1)
    projected(2)
    turned(2)
    give(1)
    projected(3)
    turned(3)
    relay(0)
    give(2)
    pass_on(0)
    relay(1)
    give(3)
    prepare()
    left_turn(0)
    gathered(0)
    theirs(0)
    flush(0)
    relay(2)
    pass_on(1)
    gathered(1)
    theirs(1)
    flush(1)
    relay(3)
    left_give(1)
    pass_on(2)
    gathered(2)
    theirs(2)
    flush(2)
    pass_on(3)
    gathered(3)
    theirs(3)
    flush(3)
    left_turn(1)
    mine(0)
    mine(1)
    mine(2)
    finish(0)
    mine(3)
    finish(1)
    sent()
    finish(2)
    finish(3)

    for w in range(WAVES):
        for b in range(blocks):
            sums(b, w).wait_send()


def on_device(n, x, gain, offset, lhs, rhs, pair, shift):
    rows = x.shape[0]
    chans, width = lhs.shape
    residues = x.shape[1] // chans
    resid = residues // n
    tiles = x.shape[1] // LANES
    team = n // 2
    across = team // 4
    depth = width * width
    out_chans = pair.shape[1]
    blocks = resid // WAVES
    fold = width // WAVES
    vmem = pl.BlockSpec(memory_space=pltpu.VMEM)
    args = [
        pltpu.with_memory_space_constraint(v, pltpu.HBM)
        for v in (x, gain.reshape(1, -1), offset.reshape(1, -1), lhs.T, rhs.T, pair)
    ]
    out = pl.pallas_call(
        functools.partial(kernel, n),
        out_shape=pltpu.VMEM((resid, residues, out_chans), F32),
        in_specs=[pl.BlockSpec(memory_space=pltpu.HBM)] * 6,
        out_specs=vmem,
        scratch_shapes=[
            pltpu.VMEM(x.shape, BF16),
            pltpu.VMEM((1, chans), F32),
            pltpu.VMEM((1, chans), F32),
            pltpu.VMEM((width, chans), BF16),
            pltpu.VMEM((width, chans), BF16),
            pltpu.VMEM(pair.shape, BF16),
            pltpu.SemaphoreType.DMA((5 + WAVES,)),
            pltpu.VMEM((tiles * rows, LANES), F32),
            pltpu.VMEM((WAVES * residues // LANES, fold * rows, LANES), F32),
            pltpu.VMEM((depth, out_chans), F32),
            pltpu.VMEM((WAVES * out_chans, depth // WAVES), BF16),
            pltpu.VMEM((2, team, rows, resid * width), BF16),
            pltpu.VMEM((2, team, rows, resid * width), BF16),
            pltpu.VMEM((2, resid * width, team * rows), BF16),
            pltpu.VMEM((WAVES, team, rows, fold * residues), BF16),
            pltpu.VMEM((depth // WAVES, resid * residues), BF16),
            pltpu.VMEM((WAVES, blocks, out_chans, residues), F32),
            pltpu.VMEM((WAVES, blocks, out_chans, residues), BF16),
            pltpu.VMEM((WAVES, blocks, out_chans, residues), BF16),
            pltpu.SemaphoreType.DMA((2, team)),
            pltpu.SemaphoreType.DMA((2, team)),
            pltpu.SemaphoreType.DMA((WAVES, across)),
            pltpu.SemaphoreType.DMA((WAVES, across)),
            pltpu.SemaphoreType.DMA((WAVES, across)),
            pltpu.SemaphoreType.DMA((WAVES, across)),
            pltpu.SemaphoreType.DMA((WAVES, across)),
            pltpu.SemaphoreType.DMA((WAVES, across)),
            pltpu.SemaphoreType.DMA((WAVES, 3, across)),
            pltpu.SemaphoreType.DMA((WAVES, 3, across)),
            pltpu.SemaphoreType.DMA((WAVES, blocks)),
            pltpu.SemaphoreType.DMA((WAVES, blocks)),
        ],
        compiler_params=pltpu.CompilerParams(
            collective_id=0, has_side_effects=True, vmem_limit_bytes=40 * 1024 * 1024
        ),
    )(*args)
    return (out + shift).astype(BF16)


def solution(mesh):
    in_specs = (P(("grp", "res"), None), P(), P(), P(), P(), P(), P())
    out_specs = P(("grp", "res"), None, None)
    return jax.shard_map(
        functools.partial(on_device, mesh.shape["res"]),
        mesh=mesh,
        in_specs=in_specs,
        out_specs=out_specs,
        check_vma=False,
    )
```

```python
import functools

import jax
import jax.numpy as jnp
from jax import lax
from jax.experimental import pallas as pl
from jax.experimental.pallas import tpu as pltpu
from jax.sharding import PartitionSpec as P

F32 = jnp.float32
BF16 = jnp.bfloat16
LANES = 128
WAVES = 4
BY_Y = 7
UNROLL = 8
DIRECT = 1


def dot(a, b):
    return jnp.dot(a, b, preferred_element_type=F32)


def kernel(
    n,
    x_hbm,
    gain_hbm,
    offset_hbm,
    lhs_hbm,
    rhs_hbm,
    pair_hbm,
    out_ref,
    x_ref,
    gain_ref,
    offset_ref,
    lhs_ref,
    rhs_ref,
    pair_ref,
    in_sem,
    norm_scr,
    turn_scr,
    pair_scr,
    pair_t,
    left_send,
    left_all,
    left_t,
    right_all,
    flat,
    kept,
    sum_send,
    sum_recv,
    l_send,
    l_recv,
    own_send,
    own_recv,
    y_send,
    y_recv,
    z_send,
    z_recv,
    peer_send,
    peer_recv,
    s_send,
    s_recv,
):
    rows = x_ref.shape[0]
    width, chans = lhs_ref.shape
    residues = x_ref.shape[1] // chans
    resid = residues // n
    tiles = x_ref.shape[1] // LANES
    per_tile = LANES // chans
    team = n // 2
    across = team // 4
    me = lax.axis_index("res")
    half = me // team
    seat = lax.rem(me, team)
    core = lax.rem(seat, 2)
    y = lax.rem(seat // 2, 2)
    z = seat // 4
    base = half * team
    partner = (1 - half) * team + seat
    peer_seat = seat + 1 - 2 * core
    late = jnp.logical_and(half == 1, 2 * z >= across)
    last_late = jnp.logical_and(half == 1, 2 * z >= across)

    def to(dev):
        return dict(device_id={"res": dev}, device_id_type=pl.DeviceIdType.MESH)

    def seat_at(z_step, flip, c):
        return lax.rem(z + z_step + across, across) * 4 + (1 - y if flip else y) * 2 + c

    barrier = pltpu.get_barrier_semaphore()

    def over(first, last, act):
        if last - first <= UNROLL:
            for k in range(first, last):
                act(k)
            return

        def step(k, carry):
            act(k)
            return carry

        lax.fori_loop(first, last, step, 0)

    def in_fours(count, act):
        step = max(k for k in (1, 2, 4) if count % k == 0)

        def some(b):
            for u in range(step):
                act(b * step + u)

        over(0, count // step, some)

    over(1, team, lambda k: pl.semaphore_signal(barrier, inc=1, **to(base + lax.rem(seat + k, team))))
    pl.semaphore_signal(barrier, inc=1, **to(partner))

    def load(k, source, target):
        copy = pltpu.make_async_copy(source, target, in_sem.at[k])
        copy.start()
        return copy

    def x_part(w):
        wide = x_ref.shape[1] // WAVES
        side = half if 2 * w >= WAVES else 1 - half
        at = pl.multiple_of((side * (WAVES // 2) + w % (WAVES // 2)) * wide, LANES)
        return x_hbm.at[:, pl.ds(at, wide)], x_ref.at[:, pl.ds(at, wide)]

    x_in = [load(4, *x_part(0))]
    small = [
        load(0, gain_hbm, gain_ref),
        load(1, offset_hbm, offset_ref),
        load(2, lhs_hbm, lhs_ref),
        load(3, rhs_hbm, rhs_ref),
    ]
    x_in += [load(4 + w, *x_part(w)) for w in range(1, WAVES)]
    pair_in = load(4 + WAVES, pair_hbm, pair_ref)
    for copy in small:
        copy.wait()

    def same(shape, down, across):
        r = lax.broadcasted_iota(jnp.int32, shape, 0) // down
        c = lax.broadcasted_iota(jnp.int32, shape, 1) // across
        return r == c

    reps = LANES // width
    lhs = jnp.concatenate([lhs_ref[...].astype(F32)] * per_tile, axis=1)
    lhs = jnp.concatenate([lhs] * reps, axis=0).T
    lhs_wide = jnp.concatenate([lhs] * (reps // per_tile), axis=0)
    lhs_wide = jnp.where(same(lhs_wide.shape, chans, width), lhs_wide, 0.0).astype(BF16)
    fold = width // WAVES
    rhs = rhs_ref[...].astype(F32)
    rhs_t = jnp.concatenate(
        [
            jnp.concatenate([rhs[k * fold : (k + 1) * fold] for k in (2 * g, 2 * g + 1)], axis=1)
            for g in range(WAVES // 2)
        ],
        axis=0,
    ).astype(BF16)
    averager = jnp.where(same((LANES, LANES), chans, chans), 1.0 / chans, 0.0).astype(BF16)
    gain = jnp.concatenate([gain_ref[...]] * per_tile, axis=1)
    offset = jnp.concatenate([offset_ref[...]] * per_tile, axis=1)

    group = 8
    dests = group * per_tile // resid
    halves = resid * width // LANES
    groups = tiles // 2 // group

    def project(b, which):
        start = ((half if which else 1 - half) * groups + b) * group
        x = jnp.concatenate(
            [
                x_ref[:, pl.ds(pl.multiple_of((start + u) * LANES, LANES), LANES)].astype(F32)
                for u in range(group)
            ],
            axis=0,
        )
        center = x - dot(x.astype(BF16), averager)
        square = center * center
        high = square.astype(BF16)
        low = (square - high.astype(F32)).astype(BF16)
        spread = dot(high, averager) + dot(low, averager)
        normed = (center * lax.rsqrt(spread + 1e-05) * gain + offset).astype(BF16)
        wide = normed.astype(F32)
        at = (which * groups + b) * group * rows
        norm_scr[pl.ds(pl.multiple_of(at, 8), group * rows), :] = wide
        even = jnp.concatenate(
            [wide[u * rows : (u + 1) * rows] for u in range(0, group, 2)], axis=0
        ).astype(BF16)
        odd = jnp.concatenate(
            [wide[u * rows : (u + 1) * rows] for u in range(1, group, 2)], axis=0
        ).astype(BF16)
        left = dot(jnp.concatenate([even, odd], axis=1), lhs_wide)
        for u in range(group // 2):
            left_send[
                which, b * dests + u // halves, :, (u % halves) * LANES : (u % halves + 1) * LANES
            ] = left[u * rows : (u + 1) * rows].astype(BF16)

    def projected(w):
        x_in[w].wait()
        count = groups // (WAVES // 2)
        in_fours(count, lambda b: project(w % (WAVES // 2) * count + b, w // (WAVES // 2)))

    def left_copy(k, which, incoming):
        slot = team - k if incoming else k
        other = lax.rem(seat + k, team)
        return pltpu.make_async_remote_copy(
            src_ref=left_send.at[which, other],
            dst_ref=left_all.at[which, other if incoming else seat],
            send_sem=l_send.at[which, slot],
            recv_sem=l_recv.at[which, slot],
            **to(base + other),
        )

    part = fold * residues
    cut = part // LANES * BY_Y // 8 * LANES

    def own(w, k, incoming):
        flip = isinstance(k, int) and k == 0
        z_step = 0 if flip else (-k if incoming else k)
        other = seat_at(z_step, flip, core)
        ref = right_all.at[w, other if incoming else seat]
        return pltpu.make_async_remote_copy(
            src_ref=ref,
            dst_ref=ref,
            send_sem=own_send.at[w, k],
            recv_sem=own_recv.at[w, k],
            **to(base + other),
        )

    def relay_y(w, k, incoming):
        source = seat_at(-k, incoming, core)
        ref = right_all.at[w, source, :, pl.ds(0, cut)]
        return pltpu.make_async_remote_copy(
            src_ref=ref,
            dst_ref=ref,
            send_sem=y_send.at[w, k],
            recv_sem=y_recv.at[w, k],
            **to(base + seat_at(0, True, core)),
        )

    def relay_z(w, k, incoming):
        source = seat_at(-k if incoming else 0, True, core)
        ref = right_all.at[w, source, :, pl.ds(cut, part - cut)]
        return pltpu.make_async_remote_copy(
            src_ref=ref,
            dst_ref=ref,
            send_sem=z_send.at[w, k],
            recv_sem=z_recv.at[w, k],
            **to(base + seat_at(-k if incoming else k, False, core)),
        )

    def far(w, k, incoming):
        other = seat_at(-k if incoming else k, True, core)
        ref = right_all.at[w, other if incoming else seat]
        return pltpu.make_async_remote_copy(
            src_ref=ref,
            dst_ref=ref,
            send_sem=z_send.at[w, k],
            recv_sem=z_recv.at[w, k],
            **to(base + other),
        )

    def share(w, k, kind, incoming):
        source = seat_at(-k, kind > 0, 1 - core if incoming else core)
        ref = right_all.at[w, source]
        if kind == 1 and w >= DIRECT:
            ref = right_all.at[w, source, :, pl.ds(0, cut)]
        if kind == 2:
            ref = right_all.at[w, source, :, pl.ds(cut, part - cut)]
        return pltpu.make_async_remote_copy(
            src_ref=ref,
            dst_ref=ref,
            send_sem=peer_send.at[w, kind, k],
            recv_sem=peer_recv.at[w, kind, k],
            **to(base + peer_seat),
        )

    def share_near(w, incoming):
        source = seat_at(0, True, 1 - core if incoming else core)
        ref = right_all.at[w, source]
        return pltpu.make_async_remote_copy(
            src_ref=ref,
            dst_ref=ref,
            send_sem=peer_send.at[w, 1, 0],
            recv_sem=peer_recv.at[w, 1, 0],
            **to(base + peer_seat),
        )

    lane = lax.broadcasted_iota(jnp.int32, (tiles // WAVES, LANES), 1) // chans
    strips = residues // LANES
    wave_tiles = tiles // WAVES
    span = residues // WAVES
    batch = 8
    fold_lane = lax.broadcasted_iota(jnp.int32, (fold, LANES), 1) // (LANES // 2)

    def turn(b, w):
        ones = [
            norm_scr[pl.ds(w * wave_tiles * rows + b * batch + v, wave_tiles, stride=rows), :]
            for v in range(batch)
        ]
        picked = []
        for one in ones:
            rolled = pltpu.roll(one, chans, 1)
            picked += [jnp.where(lane == q, one if q == h else rolled, 0.0) for q in range(2) for h in range(2)]
        spread_out = jnp.concatenate(picked, axis=0).astype(BF16)
        res = lax.dot_general(
            rhs_t, spread_out, (((1,), (1,)), ((), ())), preferred_element_type=F32
        )
        deep = residues // 2

        def put(v, j, value):
            turn_scr[w * strips + j, pl.ds(b * batch + v, fold, stride=rows), :] = value

        if deep % LANES:
            for v in range(0, batch, 2):
                low = res[:fold, v * deep : v * deep + LANES]
                high = res[fold:, v * deep : v * deep + LANES]
                put(v, 0, jnp.where(fold_lane == 0, low, pltpu.roll(high, LANES // 2, 1)))
                put(v + 1, 0, jnp.where(fold_lane == 0, pltpu.roll(low, LANES // 2, 1), high))
        else:
            for v in range(batch):
                for j in range(strips):
                    g, at = j * LANES // deep, v * deep + j * LANES % deep
                    put(v, j, res[g * fold : (g + 1) * fold, at : at + LANES])

    def turned(w):
        in_fours(rows // batch, lambda b: turn(b, w))
        for q in range(fold):
            for j in range(strips):
                at = q * residues + j * LANES
                right_all[w, seat, :, at : at + LANES] = turn_scr[
                    w * strips + j, q * rows : (q + 1) * rows, :
                ].astype(BF16)

    def give(w):
        own(w, 0, False).start()
        over(1, across, lambda k: own(w, k, False).start())
        share(w, 0, 0, False).start()
        if w < DIRECT:
            over(1, across, lambda k: far(w, k, False).start())

    def relay(w):
        def along(k):
            own(w, k, True).wait_recv()
            if w >= DIRECT:
                relay_y(w, k, False).start()
            share(w, k, 0, False).start()

        own(w, 0, True).wait_recv()
        if w >= DIRECT:
            over(1, across, lambda k: relay_z(w, k, False).start())
        share_near(w, False).start()
        over(1, across, along)

    def pass_on(w):
        def along(k):
            if w < DIRECT:
                far(w, k, True).wait_recv()
                share(w, k, 1, False).start()
                return
            relay_y(w, k, True).wait_recv()
            share(w, k, 1, False).start()
            relay_z(w, k, True).wait_recv()
            share(w, k, 2, False).start()

        over(1, across, along)

    def gathered(w):
        over(0, across, lambda k: share(w, k, 0, True).wait_recv())
        share_near(w, True).wait_recv()

        def along(k):
            share(w, k, 1, True).wait_recv()
            if w >= DIRECT:
                share(w, k, 2, True).wait_recv()

        over(1, across, along)

    out_chans = pair_ref.shape[1]

    def prepare():
        pair_in.wait()
        pair_scr[...] = pair_ref[...].astype(F32)
        for c in range(WAVES):
            for b in range(fold // reps):
                some = jnp.concatenate(
                    [
                        pair_scr[pl.ds(c * fold + b * reps + u, width, stride=width), :]
                        for u in range(reps)
                    ],
                    axis=0,
                )
                pair_t[c * out_chans : (c + 1) * out_chans, b * LANES : (b + 1) * LANES] = (
                    some.T.astype(BF16)
                )

    qs = 4
    here_rows = team * rows
    total = n * rows
    slot = lax.broadcasted_iota(jnp.int32, (out_chans, residues), 1) // span

    def fill(which, w):
        for b in range(fold // qs):
            here = right_all[w, :, :, b * qs * residues : (b + 1) * qs * residues]
            if rows % 16:
                here = here.astype(F32)
            here = here.reshape(here_rows, qs * residues).astype(BF16)
            product = (dot(left_t[which], here) * (1.0 / total)).astype(BF16)
            for u in range(qs):
                for i in range(resid):
                    flat[
                        (b * qs + u) * width : (b * qs + u + 1) * width,
                        i * residues : (i + 1) * residues,
                    ] = product[i * width : (i + 1) * width, u * residues : (u + 1) * residues]

    def sums(b, w):
        return pltpu.make_async_remote_copy(
            src_ref=sum_send.at[w, b],
            dst_ref=sum_recv.at[w, b],
            send_sem=s_send.at[w, b],
            recv_sem=s_recv.at[w, b],
            **to(partner),
        )

    def mapped(b):
        both = dot(
            pair_t[...], flat[:, b * WAVES * residues : (b + 1) * WAVES * residues]
        )
        whole = None
        for d in range(WAVES):
            one = None
            for q in range(WAVES):
                i = (q + d) % WAVES
                piece = both[q * out_chans : (q + 1) * out_chans, i * residues : (i + 1) * residues]
                one = piece if one is None else jnp.where(slot == q, piece, one)
            if d:
                one = pltpu.roll(one, d * span, 1)
            whole = one if whole is None else whole + one
        return whole

    blocks = resid // WAVES

    def theirs(w):
        fill(0, w)
        for b in range(blocks):
            sum_send[w, b] = mapped(b).astype(BF16)

            @pl.when(jnp.logical_not(last_late if w == WAVES - 1 else late))
            def _():
                sums(b, w).start()

    def flush(w):
        @pl.when(last_late if w == WAVES - 1 else late)
        def _():
            for b in range(blocks):
                sums(b, w).start()

    def mine(w):
        fill(1, w)
        for b in range(blocks):
            kept[w, b] = mapped(b)

    def finish(r):
        w = (r + WAVES // 2) % WAVES
        first = (half if 2 * w >= WAVES else 1 - half) * (residues // 2) + w % (WAVES // 2) * span
        for b in range(blocks):
            sums(b, r).wait_recv()
            done = (kept[w, b] + sum_recv[r, b].astype(F32)).T
            for u in range(WAVES):
                for h in range(2):
                    at = u * span + h * wave_tiles
                    out_ref[WAVES * b + u, pl.ds(first + h, wave_tiles, stride=2), :] = done[
                        at : at + wave_tiles
                    ]

    def left_turn(which):
        over(1, team, lambda k: left_copy(k, which, True).wait_recv())
        left_t[which] = (
            left_all[which].astype(F32).reshape(team * rows, resid * width).T.astype(BF16)
        )

    def left_give(which):
        over(1, team, lambda k: left_copy(k, which, False).start())
        left_all[which, seat] = left_send[which, seat]

    def sent():
        for w in range(WAVES):
            own(w, 0, False).wait_send()
            over(1, across, lambda k: own(w, k, False).wait_send())
            if w < DIRECT:
                over(1, across, lambda k: far(w, k, False).wait_send())
            else:
                over(1, across, lambda k: relay_y(w, k, False).wait_send())
                over(1, across, lambda k: relay_z(w, k, False).wait_send())
            over(0, across, lambda k: share(w, k, 0, False).wait_send())
            share_near(w, False).wait_send()
            over(1, across, lambda k: share(w, k, 1, False).wait_send())
            if w >= DIRECT:
                over(1, across, lambda k: share(w, k, 2, False).wait_send())
        for which in range(2):
            over(1, team, lambda k: left_copy(k, which, False).wait_send())

    projected(0)
    turned(0)
    pl.semaphore_wait(barrier, team)
    give(0)
    projected(1)
    left_give(0)
    turned(1)
    projected(2)
    turned(2)
    give(1)
    projected(3)
    turned(3)
    relay(0)
    give(2)
    pass_on(0)
    relay(1)
    give(3)
    prepare()
    left_turn(0)
    gathered(0)
    theirs(0)
    relay(2)
    flush(0)
    pass_on(1)
    gathered(1)
    theirs(1)
    flush(1)
    relay(3)
    left_give(1)
    pass_on(2)
    gathered(2)
    theirs(2)
    flush(2)
    pass_on(3)
    gathered(3)
    theirs(3)
    flush(3)
    left_turn(1)
    mine(0)
    mine(1)
    mine(2)
    finish(0)
    mine(3)
    finish(1)
    sent()
    finish(2)
    finish(3)

    for w in range(WAVES):
        for b in range(blocks):
            sums(b, w).wait_send()


def on_device(n, x, gain, offset, lhs, rhs, pair, shift):
    rows = x.shape[0]
    chans, width = lhs.shape
    residues = x.shape[1] // chans
    resid = residues // n
    tiles = x.shape[1] // LANES
    team = n // 2
    across = team // 4
    depth = width * width
    out_chans = pair.shape[1]
    blocks = resid // WAVES
    fold = width // WAVES
    vmem = pl.BlockSpec(memory_space=pltpu.VMEM)
    args = [
        pltpu.with_memory_space_constraint(v, pltpu.HBM)
        for v in (x, gain.reshape(1, -1), offset.reshape(1, -1), lhs.T, rhs.T, pair)
    ]
    out = pl.pallas_call(
        functools.partial(kernel, n),
        out_shape=pltpu.VMEM((resid, residues, out_chans), F32),
        in_specs=[pl.BlockSpec(memory_space=pltpu.HBM)] * 6,
        out_specs=vmem,
        scratch_shapes=[
            pltpu.VMEM(x.shape, BF16),
            pltpu.VMEM((1, chans), F32),
            pltpu.VMEM((1, chans), F32),
            pltpu.VMEM((width, chans), BF16),
            pltpu.VMEM((width, chans), BF16),
            pltpu.VMEM(pair.shape, BF16),
            pltpu.SemaphoreType.DMA((5 + WAVES,)),
            pltpu.VMEM((tiles * rows, LANES), F32),
            pltpu.VMEM((WAVES * residues // LANES, fold * rows, LANES), F32),
            pltpu.VMEM((depth, out_chans), F32),
            pltpu.VMEM((WAVES * out_chans, depth // WAVES), BF16),
            pltpu.VMEM((2, team, rows, resid * width), BF16),
            pltpu.VMEM((2, team, rows, resid * width), BF16),
            pltpu.VMEM((2, resid * width, team * rows), BF16),
            pltpu.VMEM((WAVES, team, rows, fold * residues), BF16),
            pltpu.VMEM((depth // WAVES, resid * residues), BF16),
            pltpu.VMEM((WAVES, blocks, out_chans, residues), F32),
            pltpu.VMEM((WAVES, blocks, out_chans, residues), BF16),
            pltpu.VMEM((WAVES, blocks, out_chans, residues), BF16),
            pltpu.SemaphoreType.DMA((2, team)),
            pltpu.SemaphoreType.DMA((2, team)),
            pltpu.SemaphoreType.DMA((WAVES, across)),
            pltpu.SemaphoreType.DMA((WAVES, across)),
            pltpu.SemaphoreType.DMA((WAVES, across)),
            pltpu.SemaphoreType.DMA((WAVES, across)),
            pltpu.SemaphoreType.DMA((WAVES, across)),
            pltpu.SemaphoreType.DMA((WAVES, across)),
            pltpu.SemaphoreType.DMA((WAVES, 3, across)),
            pltpu.SemaphoreType.DMA((WAVES, 3, across)),
            pltpu.SemaphoreType.DMA((WAVES, blocks)),
            pltpu.SemaphoreType.DMA((WAVES, blocks)),
        ],
        compiler_params=pltpu.CompilerParams(
            collective_id=0, has_side_effects=True, vmem_limit_bytes=40 * 1024 * 1024
        ),
    )(*args)
    return (out + shift).astype(BF16)


def solution(mesh):
    in_specs = (P(("grp", "res"), None), P(), P(), P(), P(), P(), P())
    out_specs = P(("grp", "res"), None, None)
    return jax.shard_map(
        functools.partial(on_device, mesh.shape["res"]),
        mesh=mesh,
        in_specs=in_specs,
        out_specs=out_specs,
        check_vma=False,
    )
```

```python
import functools

import jax
import jax.numpy as jnp
from jax import lax
from jax.experimental import pallas as pl
from jax.experimental.pallas import tpu as pltpu
from jax.sharding import PartitionSpec as P

F32 = jnp.float32
BF16 = jnp.bfloat16
LANES = 128
WAVES = 4
BY_Y = 7
UNROLL = 8
DIRECT = 2


def dot(a, b):
    return jnp.dot(a, b, preferred_element_type=F32)


def kernel(
    n,
    x_hbm,
    gain_hbm,
    offset_hbm,
    lhs_hbm,
    rhs_hbm,
    pair_hbm,
    out_ref,
    x_ref,
    gain_ref,
    offset_ref,
    lhs_ref,
    rhs_ref,
    pair_ref,
    in_sem,
    norm_scr,
    turn_scr,
    pair_scr,
    pair_t,
    left_send,
    left_all,
    left_t,
    right_all,
    flat,
    kept,
    sum_send,
    sum_recv,
    l_send,
    l_recv,
    own_send,
    own_recv,
    y_send,
    y_recv,
    z_send,
    z_recv,
    peer_send,
    peer_recv,
    s_send,
    s_recv,
):
    rows = x_ref.shape[0]
    width, chans = lhs_ref.shape
    residues = x_ref.shape[1] // chans
    resid = residues // n
    tiles = x_ref.shape[1] // LANES
    per_tile = LANES // chans
    team = n // 2
    across = team // 4
    me = lax.axis_index("res")
    half = me // team
    seat = lax.rem(me, team)
    core = lax.rem(seat, 2)
    y = lax.rem(seat // 2, 2)
    z = seat // 4
    base = half * team
    partner = (1 - half) * team + seat
    peer_seat = seat + 1 - 2 * core
    late = jnp.logical_and(half == 1, 2 * z >= across)
    last_late = jnp.logical_and(half == 1, 2 * z >= across)

    def to(dev):
        return dict(device_id={"res": dev}, device_id_type=pl.DeviceIdType.MESH)

    def seat_at(z_step, flip, c):
        return lax.rem(z + z_step + across, across) * 4 + (1 - y if flip else y) * 2 + c

    barrier = pltpu.get_barrier_semaphore()

    def over(first, last, act):
        if last - first <= UNROLL:
            for k in range(first, last):
                act(k)
            return

        def step(k, carry):
            act(k)
            return carry

        lax.fori_loop(first, last, step, 0)

    def in_fours(count, act):
        step = max(k for k in (1, 2, 4) if count % k == 0)

        def some(b):
            for u in range(step):
                act(b * step + u)

        over(0, count // step, some)

    over(1, team, lambda k: pl.semaphore_signal(barrier, inc=1, **to(base + lax.rem(seat + k, team))))
    pl.semaphore_signal(barrier, inc=1, **to(partner))

    def load(k, source, target):
        copy = pltpu.make_async_copy(source, target, in_sem.at[k])
        copy.start()
        return copy

    def x_part(w):
        wide = x_ref.shape[1] // WAVES
        side = half if 2 * w >= WAVES else 1 - half
        at = pl.multiple_of((side * (WAVES // 2) + w % (WAVES // 2)) * wide, LANES)
        return x_hbm.at[:, pl.ds(at, wide)], x_ref.at[:, pl.ds(at, wide)]

    x_in = [load(4, *x_part(0))]
    small = [
        load(0, gain_hbm, gain_ref),
        load(1, offset_hbm, offset_ref),
        load(2, lhs_hbm, lhs_ref),
        load(3, rhs_hbm, rhs_ref),
    ]
    x_in += [load(4 + w, *x_part(w)) for w in range(1, WAVES)]
    pair_in = load(4 + WAVES, pair_hbm, pair_ref)
    for copy in small:
        copy.wait()

    def same(shape, down, across):
        r = lax.broadcasted_iota(jnp.int32, shape, 0) // down
        c = lax.broadcasted_iota(jnp.int32, shape, 1) // across
        return r == c

    reps = LANES // width
    lhs = jnp.concatenate([lhs_ref[...].astype(F32)] * per_tile, axis=1)
    lhs = jnp.concatenate([lhs] * reps, axis=0).T
    lhs_wide = jnp.concatenate([lhs] * (reps // per_tile), axis=0)
    lhs_wide = jnp.where(same(lhs_wide.shape, chans, width), lhs_wide, 0.0).astype(BF16)
    fold = width // WAVES
    rhs = rhs_ref[...].astype(F32)
    rhs_t = jnp.concatenate(
        [
            jnp.concatenate([rhs[k * fold : (k + 1) * fold] for k in (2 * g, 2 * g + 1)], axis=1)
            for g in range(WAVES // 2)
        ],
        axis=0,
    ).astype(BF16)
    averager = jnp.where(same((LANES, LANES), chans, chans), 1.0 / chans, 0.0).astype(BF16)
    gain = jnp.concatenate([gain_ref[...]] * per_tile, axis=1)
    offset = jnp.concatenate([offset_ref[...]] * per_tile, axis=1)

    group = 8
    dests = group * per_tile // resid
    halves = resid * width // LANES
    groups = tiles // 2 // group

    def project(b, which):
        start = ((half if which else 1 - half) * groups + b) * group
        x = jnp.concatenate(
            [
                x_ref[:, pl.ds(pl.multiple_of((start + u) * LANES, LANES), LANES)].astype(F32)
                for u in range(group)
            ],
            axis=0,
        )
        center = x - dot(x.astype(BF16), averager)
        square = center * center
        high = square.astype(BF16)
        low = (square - high.astype(F32)).astype(BF16)
        spread = dot(high, averager) + dot(low, averager)
        normed = (center * lax.rsqrt(spread + 1e-05) * gain + offset).astype(BF16)
        wide = normed.astype(F32)
        at = (which * groups + b) * group * rows
        norm_scr[pl.ds(pl.multiple_of(at, 8), group * rows), :] = wide
        even = jnp.concatenate(
            [wide[u * rows : (u + 1) * rows] for u in range(0, group, 2)], axis=0
        ).astype(BF16)
        odd = jnp.concatenate(
            [wide[u * rows : (u + 1) * rows] for u in range(1, group, 2)], axis=0
        ).astype(BF16)
        left = dot(jnp.concatenate([even, odd], axis=1), lhs_wide)
        for u in range(group // 2):
            left_send[
                which, b * dests + u // halves, :, (u % halves) * LANES : (u % halves + 1) * LANES
            ] = left[u * rows : (u + 1) * rows].astype(BF16)

    def projected(w):
        x_in[w].wait()
        count = groups // (WAVES // 2)
        in_fours(count, lambda b: project(w % (WAVES // 2) * count + b, w // (WAVES // 2)))

    def left_copy(k, which, incoming):
        slot = team - k if incoming else k
        other = lax.rem(seat + k, team)
        return pltpu.make_async_remote_copy(
            src_ref=left_send.at[which, other],
            dst_ref=left_all.at[which, other if incoming else seat],
            send_sem=l_send.at[which, slot],
            recv_sem=l_recv.at[which, slot],
            **to(base + other),
        )

    part = fold * residues
    cut = part // LANES * BY_Y // 8 * LANES

    def own(w, k, incoming):
        flip = isinstance(k, int) and k == 0
        z_step = 0 if flip else (-k if incoming else k)
        other = seat_at(z_step, flip, core)
        ref = right_all.at[w, other if incoming else seat]
        return pltpu.make_async_remote_copy(
            src_ref=ref,
            dst_ref=ref,
            send_sem=own_send.at[w, k],
            recv_sem=own_recv.at[w, k],
            **to(base + other),
        )

    def relay_y(w, k, incoming):
        source = seat_at(-k, incoming, core)
        ref = right_all.at[w, source, :, pl.ds(0, cut)]
        return pltpu.make_async_remote_copy(
            src_ref=ref,
            dst_ref=ref,
            send_sem=y_send.at[w, k],
            recv_sem=y_recv.at[w, k],
            **to(base + seat_at(0, True, core)),
        )

    def relay_z(w, k, incoming):
        source = seat_at(-k if incoming else 0, True, core)
        ref = right_all.at[w, source, :, pl.ds(cut, part - cut)]
        return pltpu.make_async_remote_copy(
            src_ref=ref,
            dst_ref=ref,
            send_sem=z_send.at[w, k],
            recv_sem=z_recv.at[w, k],
            **to(base + seat_at(-k if incoming else k, False, core)),
        )

    def far(w, k, incoming):
        other = seat_at(-k if incoming else k, True, core)
        ref = right_all.at[w, other if incoming else seat]
        return pltpu.make_async_remote_copy(
            src_ref=ref,
            dst_ref=ref,
            send_sem=z_send.at[w, k],
            recv_sem=z_recv.at[w, k],
            **to(base + other),
        )

    def share(w, k, kind, incoming):
        source = seat_at(-k, kind > 0, 1 - core if incoming else core)
        ref = right_all.at[w, source]
        if kind == 1 and w >= DIRECT:
            ref = right_all.at[w, source, :, pl.ds(0, cut)]
        if kind == 2:
            ref = right_all.at[w, source, :, pl.ds(cut, part - cut)]
        return pltpu.make_async_remote_copy(
            src_ref=ref,
            dst_ref=ref,
            send_sem=peer_send.at[w, kind, k],
            recv_sem=peer_recv.at[w, kind, k],
            **to(base + peer_seat),
        )

    def share_near(w, incoming):
        source = seat_at(0, True, 1 - core if incoming else core)
        ref = right_all.at[w, source]
        return pltpu.make_async_remote_copy(
            src_ref=ref,
            dst_ref=ref,
            send_sem=peer_send.at[w, 1, 0],
            recv_sem=peer_recv.at[w, 1, 0],
            **to(base + peer_seat),
        )

    lane = lax.broadcasted_iota(jnp.int32, (tiles // WAVES, LANES), 1) // chans
    strips = residues // LANES
    wave_tiles = tiles // WAVES
    span = residues // WAVES
    batch = 8
    fold_lane = lax.broadcasted_iota(jnp.int32, (fold, LANES), 1) // (LANES // 2)

    def turn(b, w):
        ones = [
            norm_scr[pl.ds(w * wave_tiles * rows + b * batch + v, wave_tiles, stride=rows), :]
            for v in range(batch)
        ]
        picked = []
        for one in ones:
            rolled = pltpu.roll(one, chans, 1)
            picked += [jnp.where(lane == q, one if q == h else rolled, 0.0) for q in range(2) for h in range(2)]
        spread_out = jnp.concatenate(picked, axis=0).astype(BF16)
        res = lax.dot_general(
            rhs_t, spread_out, (((1,), (1,)), ((), ())), preferred_element_type=F32
        )
        deep = residues // 2

        def put(v, j, value):
            turn_scr[w * strips + j, pl.ds(b * batch + v, fold, stride=rows), :] = value

        if deep % LANES:
            for v in range(0, batch, 2):
                low = res[:fold, v * deep : v * deep + LANES]
                high = res[fold:, v * deep : v * deep + LANES]
                put(v, 0, jnp.where(fold_lane == 0, low, pltpu.roll(high, LANES // 2, 1)))
                put(v + 1, 0, jnp.where(fold_lane == 0, pltpu.roll(low, LANES // 2, 1), high))
        else:
            for v in range(batch):
                for j in range(strips):
                    g, at = j * LANES // deep, v * deep + j * LANES % deep
                    put(v, j, res[g * fold : (g + 1) * fold, at : at + LANES])

    def turned(w):
        in_fours(rows // batch, lambda b: turn(b, w))
        for q in range(fold):
            for j in range(strips):
                at = q * residues + j * LANES
                right_all[w, seat, :, at : at + LANES] = turn_scr[
                    w * strips + j, q * rows : (q + 1) * rows, :
                ].astype(BF16)

    def give(w):
        own(w, 0, False).start()
        over(1, across, lambda k: own(w, k, False).start())
        share(w, 0, 0, False).start()
        if w < DIRECT:
            over(1, across, lambda k: far(w, k, False).start())

    def relay(w):
        def along(k):
            own(w, k, True).wait_recv()
            if w >= DIRECT:
                relay_y(w, k, False).start()
            share(w, k, 0, False).start()

        own(w, 0, True).wait_recv()
        if w >= DIRECT:
            over(1, across, lambda k: relay_z(w, k, False).start())
        share_near(w, False).start()
        over(1, across, along)

    def pass_on(w):
        def along(k):
            if w < DIRECT:
                far(w, k, True).wait_recv()
                share(w, k, 1, False).start()
                return
            relay_y(w, k, True).wait_recv()
            share(w, k, 1, False).start()
            relay_z(w, k, True).wait_recv()
            share(w, k, 2, False).start()

        over(1, across, along)

    def gathered(w):
        over(0, across, lambda k: share(w, k, 0, True).wait_recv())
        share_near(w, True).wait_recv()

        def along(k):
            share(w, k, 1, True).wait_recv()
            if w >= DIRECT:
                share(w, k, 2, True).wait_recv()

        over(1, across, along)

    out_chans = pair_ref.shape[1]

    def prepare():
        pair_in.wait()
        pair_scr[...] = pair_ref[...].astype(F32)
        for c in range(WAVES):
            for b in range(fold // reps):
                some = jnp.concatenate(
                    [
                        pair_scr[pl.ds(c * fold + b * reps + u, width, stride=width), :]
                        for u in range(reps)
                    ],
                    axis=0,
                )
                pair_t[c * out_chans : (c + 1) * out_chans, b * LANES : (b + 1) * LANES] = (
                    some.T.astype(BF16)
                )

    qs = 4
    here_rows = team * rows
    total = n * rows
    slot = lax.broadcasted_iota(jnp.int32, (out_chans, residues), 1) // span

    def fill(which, w):
        for b in range(fold // qs):
            here = right_all[w, :, :, b * qs * residues : (b + 1) * qs * residues]
            if rows % 16:
                here = here.astype(F32)
            here = here.reshape(here_rows, qs * residues).astype(BF16)
            product = (dot(left_t[which], here) * (1.0 / total)).astype(BF16)
            for u in range(qs):
                for i in range(resid):
                    flat[
                        (b * qs + u) * width : (b * qs + u + 1) * width,
                        i * residues : (i + 1) * residues,
                    ] = product[i * width : (i + 1) * width, u * residues : (u + 1) * residues]

    def sums(b, w):
        return pltpu.make_async_remote_copy(
            src_ref=sum_send.at[w, b],
            dst_ref=sum_recv.at[w, b],
            send_sem=s_send.at[w, b],
            recv_sem=s_recv.at[w, b],
            **to(partner),
        )

    def mapped(b):
        both = dot(
            pair_t[...], flat[:, b * WAVES * residues : (b + 1) * WAVES * residues]
        )
        whole = None
        for d in range(WAVES):
            one = None
            for q in range(WAVES):
                i = (q + d) % WAVES
                piece = both[q * out_chans : (q + 1) * out_chans, i * residues : (i + 1) * residues]
                one = piece if one is None else jnp.where(slot == q, piece, one)
            if d:
                one = pltpu.roll(one, d * span, 1)
            whole = one if whole is None else whole + one
        return whole

    blocks = resid // WAVES

    def theirs(w):
        fill(0, w)
        for b in range(blocks):
            sum_send[w, b] = mapped(b).astype(BF16)

            @pl.when(jnp.logical_not(last_late if w == WAVES - 1 else late))
            def _():
                sums(b, w).start()

    def flush(w):
        @pl.when(last_late if w == WAVES - 1 else late)
        def _():
            for b in range(blocks):
                sums(b, w).start()

    def mine(w):
        fill(1, w)
        for b in range(blocks):
            kept[w, b] = mapped(b)

    def finish(r):
        w = (r + WAVES // 2) % WAVES
        first = (half if 2 * w >= WAVES else 1 - half) * (residues // 2) + w % (WAVES // 2) * span
        for b in range(blocks):
            sums(b, r).wait_recv()
            done = (kept[w, b] + sum_recv[r, b].astype(F32)).T
            for u in range(WAVES):
                for h in range(2):
                    at = u * span + h * wave_tiles
                    out_ref[WAVES * b + u, pl.ds(first + h, wave_tiles, stride=2), :] = done[
                        at : at + wave_tiles
                    ]

    def left_turn(which):
        over(1, team, lambda k: left_copy(k, which, True).wait_recv())
        left_t[which] = (
            left_all[which].astype(F32).reshape(team * rows, resid * width).T.astype(BF16)
        )

    def left_give(which):
        over(1, team, lambda k: left_copy(k, which, False).start())
        left_all[which, seat] = left_send[which, seat]

    def sent():
        for w in range(WAVES):
            own(w, 0, False).wait_send()
            over(1, across, lambda k: own(w, k, False).wait_send())
            if w < DIRECT:
                over(1, across, lambda k: far(w, k, False).wait_send())
            else:
                over(1, across, lambda k: relay_y(w, k, False).wait_send())
                over(1, across, lambda k: relay_z(w, k, False).wait_send())
            over(0, across, lambda k: share(w, k, 0, False).wait_send())
            share_near(w, False).wait_send()
            over(1, across, lambda k: share(w, k, 1, False).wait_send())
            if w >= DIRECT:
                over(1, across, lambda k: share(w, k, 2, False).wait_send())
        for which in range(2):
            over(1, team, lambda k: left_copy(k, which, False).wait_send())

    projected(0)
    turned(0)
    pl.semaphore_wait(barrier, team)
    give(0)
    projected(1)
    left_give(0)
    turned(1)
    projected(2)
    turned(2)
    give(1)
    projected(3)
    turned(3)
    relay(0)
    give(2)
    pass_on(0)
    relay(1)
    give(3)
    prepare()
    left_turn(0)
    gathered(0)
    theirs(0)
    relay(2)
    flush(0)
    pass_on(1)
    gathered(1)
    theirs(1)
    flush(1)
    relay(3)
    left_give(1)
    pass_on(2)
    gathered(2)
    theirs(2)
    flush(2)
    pass_on(3)
    gathered(3)
    theirs(3)
    left_turn(1)
    flush(3)
    mine(0)
    mine(1)
    mine(2)
    finish(0)
    mine(3)
    sent()
    finish(1)
    finish(2)
    finish(3)

    for w in range(WAVES):
        for b in range(blocks):
            sums(b, w).wait_send()


def on_device(n, x, gain, offset, lhs, rhs, pair, shift):
    rows = x.shape[0]
    chans, width = lhs.shape
    residues = x.shape[1] // chans
    resid = residues // n
    tiles = x.shape[1] // LANES
    team = n // 2
    across = team // 4
    depth = width * width
    out_chans = pair.shape[1]
    blocks = resid // WAVES
    fold = width // WAVES
    vmem = pl.BlockSpec(memory_space=pltpu.VMEM)
    args = [
        pltpu.with_memory_space_constraint(v, pltpu.HBM)
        for v in (x, gain.reshape(1, -1), offset.reshape(1, -1), lhs.T, rhs.T, pair)
    ]
    out = pl.pallas_call(
        functools.partial(kernel, n),
        out_shape=pltpu.VMEM((resid, residues, out_chans), F32),
        in_specs=[pl.BlockSpec(memory_space=pltpu.HBM)] * 6,
        out_specs=vmem,
        scratch_shapes=[
            pltpu.VMEM(x.shape, BF16),
            pltpu.VMEM((1, chans), F32),
            pltpu.VMEM((1, chans), F32),
            pltpu.VMEM((width, chans), BF16),
            pltpu.VMEM((width, chans), BF16),
            pltpu.VMEM(pair.shape, BF16),
            pltpu.SemaphoreType.DMA((5 + WAVES,)),
            pltpu.VMEM((tiles * rows, LANES), F32),
            pltpu.VMEM((WAVES * residues // LANES, fold * rows, LANES), F32),
            pltpu.VMEM((depth, out_chans), F32),
            pltpu.VMEM((WAVES * out_chans, depth // WAVES), BF16),
            pltpu.VMEM((2, team, rows, resid * width), BF16),
            pltpu.VMEM((2, team, rows, resid * width), BF16),
            pltpu.VMEM((2, resid * width, team * rows), BF16),
            pltpu.VMEM((WAVES, team, rows, fold * residues), BF16),
            pltpu.VMEM((depth // WAVES, resid * residues), BF16),
            pltpu.VMEM((WAVES, blocks, out_chans, residues), F32),
            pltpu.VMEM((WAVES, blocks, out_chans, residues), BF16),
            pltpu.VMEM((WAVES, blocks, out_chans, residues), BF16),
            pltpu.SemaphoreType.DMA((2, team)),
            pltpu.SemaphoreType.DMA((2, team)),
            pltpu.SemaphoreType.DMA((WAVES, across)),
            pltpu.SemaphoreType.DMA((WAVES, across)),
            pltpu.SemaphoreType.DMA((WAVES, across)),
            pltpu.SemaphoreType.DMA((WAVES, across)),
            pltpu.SemaphoreType.DMA((WAVES, across)),
            pltpu.SemaphoreType.DMA((WAVES, across)),
            pltpu.SemaphoreType.DMA((WAVES, 3, across)),
            pltpu.SemaphoreType.DMA((WAVES, 3, across)),
            pltpu.SemaphoreType.DMA((WAVES, blocks)),
            pltpu.SemaphoreType.DMA((WAVES, blocks)),
        ],
        compiler_params=pltpu.CompilerParams(
            collective_id=0, has_side_effects=True, vmem_limit_bytes=40 * 1024 * 1024
        ),
    )(*args)
    return (out + shift).astype(BF16)


def solution(mesh):
    in_specs = (P(("grp", "res"), None), P(), P(), P(), P(), P(), P())
    out_specs = P(("grp", "res"), None, None)
    return jax.shard_map(
        functools.partial(on_device, mesh.shape["res"]),
        mesh=mesh,
        in_specs=in_specs,
        out_specs=out_specs,
        check_vma=False,
    )
```
